32 devices in a mesh: dom: 8 (over y, x, core), sub: 4 (over z).
Axes of the slice: x: 2, y: 2, z: 4, core: 2. Of those that a mesh axis runs over, the one named last changes fastest.
Arguments:
- start_dofs: float32 [140, 8192], P(None, ('dom', 'sub')), may hold values from -6 to 6
- inv_jac: float32 [9, 8192], P(None, ('dom', 'sub')), may hold values from -2 to 2
- normals: float32 [12, 8192], P(None, ('dom', 'sub')), may hold values from -3.5 to 3.5
- bulk_modulus: float32 [8192], P(('dom', 'sub')), may hold values from 0.5 to 2
- density: float32 [8192], P(('dom', 'sub')), may hold values from 0.5 to 2
- deriv_mats: float32 [3, 35, 35], replicated, may hold values from -1 to 1
- face_proj: float32 [4, 15, 35], replicated, may hold values from -1 to 1
- face_lift: float32 [4, 35, 15], replicated, may hold values from -1 to 1
- cluster: int32 [8192], P(('dom', 'sub')), may hold values from 0 to 1, as said below
- pml_flags: int32 [8192], P(('dom', 'sub')), may hold values 0 or 1
- neighbours: int32 [4, 8192], P(None, ('dom', 'sub')), may hold values from 0 to 1343, as said below
- dom_send: int32 [64, 96], P(('dom', 'sub')), may hold values from 0 to 1023, as said below
- sub_send: int32 [128, 32], P(('dom', 'sub')), may hold values from 0 to 1022, as said below
Outputs:
- final_dofs: float32 [140, 8192], P(None, ('dom', 'sub'))
The draws below stay inside these ranges and needn't reach their ends.
Inputs may be any that keep to these rules, and one draw needn't show every extreme that they name: `cluster`: on every device the fine elements come first among its 256 elements; a device holds at most 64 of them, and some device exactly 64. `neighbours`: each face names one column of its device's trace pool. Own faces that are not listed for sending name each other in pairs. The face at place j of dom_send row 0 names place j of the block from the device before, the one at place j of row 1 place j of the block from the device after; the face at place j of the sub_send row for device b names place j of the block from b, or place j + 1 - 2 (j % 2) when b is the device itself. `dom_send`: together with its sub_send rows, the rows of one device list distinct columns of its own faces; every device lists its last face column here. `sub_send`: together with its dom_send rows, the rows of one device list distinct columns of its own faces; every device lists its second-to-last face column here.
All inputs are finite; a program needn't handle non-finite values. No bound on the sum of `pml_flags` on one device may be relied on, other than what follows from the above.
Results may differ from the reference program's by a relative error of at most 0.0003.
Values sent between devices are 32-bit elements; how exact they have to be, the bound alone decides.
No kernel may reach another device: no remote copies, remote signals or barrier semaphores. Data moves between devices by JAX's collectives and lax.ppermute only.
A program may use at most 64 MiB of HBM per device.

```python
import math
import jax
import jax.numpy as jnp
from jax import lax

NQ = 4
NB = 35
NF = 15
ORDER = 5
SUBSTEPS = 4
ELEM_DEV = 256
HALO = 96
SUB_HALO = 32
FINE_CAP = 64
ELEMENTS = 8192
N_DOM = 8
N_SUB = 4
DEVICES = 32


def face_layout(key):
    n_face = 4 * ELEM_DEV
    device_keys = jax.random.split(jax.random.fold_in(key, 11), DEVICES)

    def one_device(dev_key, device):
        shuffled = jax.random.permutation(dev_key, n_face).astype(jnp.int32)
        shuffled = (shuffled - shuffled[0] + n_face - 1) % n_face
        n_dom = 2 * HALO
        n_sub = N_SUB * SUB_HALO
        spot = jnp.argmax(shuffled == n_face - 2).astype(jnp.int32)
        moved = shuffled[n_dom]
        shuffled = shuffled.at[spot].set(moved).at[n_dom].set(n_face - 2)
        dom_list = shuffled[:n_dom]
        sub_list = shuffled[n_dom:n_dom + n_sub]
        remaining = shuffled[n_dom + n_sub:].reshape(-1, 2)
        positions = jnp.arange(HALO, dtype=jnp.int32)
        dom_target = n_face + jnp.concatenate([positions, HALO + positions])
        block_ids = jnp.repeat(jnp.arange(N_SUB, dtype=jnp.int32), SUB_HALO)
        entry_ids = jnp.tile(jnp.arange(SUB_HALO, dtype=jnp.int32), N_SUB)
        partner = entry_ids + 1 - 2 * (entry_ids % 2)
        own_sub = device % N_SUB
        slot_entry = jnp.where(block_ids == own_sub, partner, entry_ids)
        sub_target = n_face + 2 * HALO + block_ids * SUB_HALO + slot_entry
        lookup_table = jnp.zeros((n_face,), jnp.int32)
        lookup_table = lookup_table.at[dom_list].set(dom_target)
        lookup_table = lookup_table.at[sub_list].set(sub_target)
        lookup_table = lookup_table.at[remaining[:, 0]].set(remaining[:, 1])
        lookup_table = lookup_table.at[remaining[:, 1]].set(remaining[:, 0])
        return (lookup_table.reshape(4, ELEM_DEV), dom_list.reshape(2, HALO), sub_list.reshape(N_SUB, SUB_HALO))
    return jax.vmap(one_device)(device_keys, jnp.arange(DEVICES, dtype=jnp.int32))


def draw_neighbours(key, part):
    lookup_all = face_layout(key)[0]
    return jnp.transpose(lookup_all, (1, 0, 2)).reshape(4, DEVICES * ELEM_DEV)


def draw_dom_send(key, part):
    return face_layout(key)[1].reshape(2 * DEVICES, HALO)


def draw_sub_send(key, part):
    return face_layout(key)[2].reshape(N_SUB * DEVICES, SUB_HALO)


def cluster_map(key):
    base_key = jax.random.fold_in(key, 23)
    key_div, key_top = jax.random.split(base_key)
    divisor = jax.random.randint(key_div, (DEVICES,), 1, 5)
    counts = FINE_CAP // divisor
    busiest = jax.random.randint(key_top, (), 0, DEVICES)
    counts = counts.at[busiest].set(FINE_CAP)
    positions = jnp.arange(ELEM_DEV, dtype=jnp.int32)
    return (positions[None, :] < counts[:, None]).astype(jnp.int32).reshape(DEVICES * ELEM_DEV)


def draw_cluster(key, part):
    return cluster_map(key)


def draw_inv_jac(key, part):
    fine_flags = cluster_map(key).astype(jnp.float32)
    size_factor = 0.25 + 0.75 * fine_flags
    jac_key = jax.random.fold_in(key, 37)
    raw_values = 0.5 * jnp.clip(jax.random.normal(jac_key, (9, ELEMENTS), jnp.float32), -4.0, 4.0)
    return raw_values * size_factor[None, :]


def place_ends(drawn, rng, least, high):
    index_at = [jax.random.randint(jax.random.fold_in(rng, axis), (), 0, length) for axis, length in enumerate(drawn.shape)]
    widest = drawn.shape.index(max(drawn.shape))
    neighbour = index_at[:widest] + [(index_at[widest] + 1) % drawn.shape[widest]] + index_at[widest + 1:]
    return drawn.at[tuple(index_at)].set(least).at[tuple(neighbour)].set(high)


def block_levels(stream_key, shape, cuts, smallest, high):
    loudness, own = 1.0, jax.random.fold_in(stream_key, 6)
    for position, shards_of in cuts:
        steps = jnp.exp(jax.random.uniform(jax.random.fold_in(own, position), (shards_of,), jnp.float32, smallest / len(cuts), high / len(cuts)))
        loudness = loudness * jnp.repeat(steps, shape[position] // shards_of).reshape([-1 if axis == position else 1 for axis in range(len(shape))])
    return loudness


def bell_draw(own_key, dims, width, limit, cuts=(), kind=jnp.bfloat16):
    factor_of = block_levels(own_key, dims, cuts, -0.22, 0.18) if cuts else 1.0
    values = jax.random.normal(own_key, dims, jnp.float32) * width * factor_of
    return jnp.minimum(jnp.maximum(values, -limit), limit).astype(kind)


def setup_inputs(seed: int = 0) -> dict:
    key_list = jax.random.split(jax.random.key(seed), 14)
    start_dofs = bell_draw(key_list[0], (NQ * NB, ELEMENTS), 1.0, 6.0, ((1, 32),), jnp.float32)
    inv_jac = draw_inv_jac(jax.random.fold_in(key_list[13], 71), 0)
    normals = bell_draw(key_list[2], (12, ELEMENTS), 0.6, 3.5, ((1, 32),), jnp.float32)
    bulk_modulus = jnp.clip(jnp.exp(math.log(2.0) - 1.3862944 * jax.random.uniform(key_list[3], (ELEMENTS,), jnp.float32) ** block_levels(key_list[3], (ELEMENTS,), ((0, 32),), -0.2, 0.2)), 0.5, 2.0)
    density = jnp.clip(jnp.exp(math.log(2.0) - 1.3862944 * jax.random.uniform(key_list[4], (ELEMENTS,), jnp.float32) ** block_levels(key_list[4], (ELEMENTS,), ((0, 32),), -0.2, 0.2)), 0.5, 2.0)
    deriv_mats = bell_draw(key_list[5], (3, NB, NB), NB ** -0.5, 1.0, (), jnp.float32)
    face_proj = bell_draw(key_list[6], (4, NF, NB), NB ** -0.5, 1.0, (), jnp.float32)
    face_lift = bell_draw(key_list[7], (4, NB, NF), (2 * NF) ** -0.5, 1.0, (), jnp.float32)
    cluster = draw_cluster(jax.random.fold_in(key_list[13], 71), 0)
    pml_flags = place_ends((jax.random.randint(key_list[9], (ELEMENTS,), 0, 4) < 1).astype(jnp.int32), jax.random.fold_in(key_list[9], 1), 0, 1)
    neighbours = draw_neighbours(jax.random.fold_in(key_list[13], 71), 0)
    dom_send = draw_dom_send(jax.random.fold_in(key_list[13], 71), 0)
    sub_send = draw_sub_send(jax.random.fold_in(key_list[13], 71), 0)
    return {"start_dofs": start_dofs, "inv_jac": inv_jac, "normals": normals, "bulk_modulus": bulk_modulus, "density": density, "deriv_mats": deriv_mats, "face_proj": face_proj, "face_lift": face_lift, "cluster": cluster, "pml_flags": pml_flags, "neighbours": neighbours, "dom_send": dom_send, "sub_send": sub_send}


exact_dots = lax.Precision.HIGHEST
step_size = 0.8
sigma_pml = 1.5

def apply_operator(coeffs, material):
    inv_jac, bulk_modulus, density, damping, deriv_mats = material
    n_basis = deriv_mats.shape[1]
    pressure = coeffs[0]
    velocity = coeffs[1:]
    stacked = deriv_mats.reshape(3 * n_basis, n_basis)
    d_press = jnp.dot(stacked, pressure, precision=exact_dots).reshape(3, n_basis, -1)
    jacobian = inv_jac.reshape(3, 3, -1)
    gradient = lax.optimization_barrier(jnp.sum(jacobian[:, :, None, :] * d_press[:, None, :, :], axis=0))
    mixed_vel = lax.optimization_barrier(jnp.sum(jacobian[:, :, None, :] * velocity[None, :, :, :], axis=1))
    joined = jnp.transpose(deriv_mats, (1, 0, 2)).reshape(n_basis, 3 * n_basis)
    diverg = jnp.dot(joined, mixed_vel.reshape(3 * n_basis, -1), precision=exact_dots)
    press_rate = -bulk_modulus * diverg - damping * pressure
    veloc_rate = -gradient / density - damping * velocity
    return jnp.concatenate([press_rate[None], veloc_rate], axis=0)

def taylor(coeffs, material):
    deriv_terms = [coeffs]
    for power in range(ORDER - 1):
        deriv_terms.append(apply_operator(deriv_terms[-1], material))
    return deriv_terms

def integrate(deriv_terms, start_time, end_time):
    summed = None
    for power, taylor_term in enumerate(deriv_terms):
        weight = (end_time ** (power + 1) - start_time ** (power + 1)) / math.factorial(power + 1)
        scaled = weight * taylor_term
        summed = scaled if summed is None else summed + scaled
    return summed

def face_traces(coeffs, face_proj):
    face_parts = []
    for face_idx in range(4):
        traced = jnp.einsum('kb,qbe->kqe', face_proj[face_idx], coeffs, precision=exact_dots)
        face_parts.append(traced.reshape(-1, coeffs.shape[2]))
    return jnp.concatenate(face_parts, axis=1)

def corrections(own_traces, nbr_traces, normals, bulk_modulus, density, face_lift):
    n_elem = normals.shape[1]
    n_face = face_lift.shape[2]
    jump_all = (nbr_traces - own_traces).reshape(n_face, 4, 4, n_elem)
    jump_press = jump_all[:, 0]
    jump_vel = jump_all[:, 1:]
    facing = jnp.transpose(normals.reshape(4, 3, n_elem), (1, 0, 2))
    normal_flow = lax.optimization_barrier(jnp.sum(facing[None] * jump_vel, axis=1))
    sound_speed = jnp.sqrt(bulk_modulus / density)
    penalty = sound_speed * jnp.sqrt(lax.optimization_barrier(jnp.sum(facing * facing, axis=0)))
    flux_press = 0.5 * (bulk_modulus * normal_flow - penalty * jump_press)
    flux_veloc = 0.5 * (facing[None] * jump_press[:, None] / density - penalty * jump_vel)
    flux_all = jnp.concatenate([flux_press[:, None], flux_veloc], axis=1)
    return jnp.einsum('fbk,kqfe->qbe', face_lift, flux_all, precision=exact_dots)

def by_device(values_all):
    regrouped = values_all.reshape(values_all.shape[:-1] + (DEVICES, ELEM_DEV))
    return jnp.moveaxis(regrouped, -2, 0)

def reference(start_dofs, inv_jac, normals, bulk_modulus, density, deriv_mats, face_proj, face_lift, cluster, pml_flags, neighbours, dom_send, sub_send):
    dofs_dev = by_device(start_dofs).reshape(DEVICES, NQ, NB, ELEM_DEV)
    jac_dev = by_device(inv_jac)
    normal_dev = by_device(normals)
    bulk_dev = by_device(bulk_modulus)
    density_dev = by_device(density)
    damping_dev = by_device(sigma_pml * pml_flags.astype(jnp.float32))
    fine_dev = by_device(cluster) == 1
    neighbour_dev = by_device(neighbours)
    dom_dev = dom_send.reshape(DEVICES, 2, HALO)
    sub_dev = sub_send.reshape(DEVICES, N_SUB, SUB_HALO)
    n_chan = NF * NQ
    sub_dt = step_size / SUBSTEPS
    work_state = jnp.where(fine_dev[:, None, None, :], dofs_dev, 0.0)
    for sub_step in range(SUBSTEPS):
        start_time = sub_step * sub_dt
        end_time = (sub_step + 1) * sub_dt

        def predict(packed):
            dofs_zero, current, jac_part, bulk_part, dens_part, damp_part, fine_mask, dom_list, sub_list = packed
            material = (jac_part, bulk_part, dens_part, damp_part, deriv_mats)
            coarse_part = integrate(taylor(dofs_zero, material), start_time, end_time)
            fine_part = integrate(taylor(current, material), 0.0, sub_dt)
            published = jnp.where(fine_mask, fine_part, coarse_part)
            own_traces = face_traces(published, face_proj)
            dom_out = jnp.stack([jnp.take(own_traces, dom_list[0], axis=1), jnp.take(own_traces, dom_list[1], axis=1)])
            sub_out = jnp.take(own_traces, sub_list.reshape(-1), axis=1).reshape(n_chan, N_SUB, SUB_HALO)
            return (published, dom_out, sub_out)
        published_all, dom_all, sub_all = lax.map(predict, (dofs_dev, work_state, jac_dev, bulk_dev, density_dev, damping_dev, fine_dev, dom_dev, sub_dev))
        dom_grid = dom_all.reshape(N_DOM, N_SUB, 2, n_chan, HALO)
        zero_block = jnp.zeros_like(dom_grid[:1, :, 0])
        from_below = jnp.concatenate([zero_block, dom_grid[:-1, :, 1]], axis=0).reshape(DEVICES, n_chan, HALO)
        from_above = jnp.concatenate([dom_grid[1:, :, 0], zero_block], axis=0).reshape(DEVICES, n_chan, HALO)
        sub_grid = sub_all.reshape(N_DOM, N_SUB, n_chan, N_SUB, SUB_HALO)
        sub_in = jnp.transpose(sub_grid, (0, 3, 2, 1, 4)).reshape(DEVICES, n_chan, N_SUB * SUB_HALO)

        def update(packed):
            published, current, jac_part, bulk_part, dens_part, damp_part, normal_part, fine_mask, neighbour_part, below_part, above_part, sub_part = packed
            material = (jac_part, bulk_part, dens_part, damp_part, deriv_mats)
            own_traces = face_traces(published, face_proj)
            trace_pool = jnp.concatenate([own_traces, below_part, above_part, sub_part], axis=1)
            nbr_traces = jnp.take(trace_pool, neighbour_part.reshape(-1), axis=1)
            lifted = corrections(own_traces, nbr_traces, normal_part, bulk_part, dens_part, face_lift)
            stepped = current + apply_operator(published, material) - lifted
            return jnp.where(fine_mask, stepped, current + lifted)
        work_state = lax.map(update, (published_all, work_state, jac_dev, bulk_dev, density_dev, damping_dev, normal_dev, fine_dev, neighbour_dev, from_below, from_above, sub_in))

    def finish_step(packed):
        dofs_zero, current, jac_part, bulk_part, dens_part, damp_part, fine_mask = packed
        material = (jac_part, bulk_part, dens_part, damp_part, deriv_mats)
        full_step = integrate(taylor(dofs_zero, material), 0.0, step_size)
        coarse_out = dofs_zero + apply_operator(full_step, material) - current
        return jnp.where(fine_mask, current, coarse_out)
    result_dofs = lax.map(finish_step, (dofs_dev, work_state, jac_dev, bulk_dev, density_dev, damping_dev, fine_dev))
    return jnp.moveaxis(result_dofs.reshape(DEVICES, NQ * NB, ELEM_DEV), 0, 1).reshape(NQ * NB, ELEMENTS)
```

```python
import math

import jax
import jax.numpy as jnp
from jax import lax
from jax.experimental import pallas as pl
from jax.experimental.pallas import tpu as pltpu
from jax.sharding import PartitionSpec as P

NQ = 4
NB = 35
NF = 15
ORDER = 5
SUBSTEPS = 4
BR = 40
KR = 16
LANES = 128

step_size = 0.8
sigma_pml = 1.5
f32 = jnp.float32
bf16 = jnp.bfloat16


def weights(start_time, end_time):
    return [
        (end_time ** (k + 1) - start_time ** (k + 1)) / math.factorial(k + 1)
        for k in range(ORDER)
    ]


SUB_DT = step_size / SUBSTEPS


def hi_lo(x):
    hi = x.astype(bf16).astype(f32)
    return hi, x - hi


def split3(x):
    hi, lo = hi_lo(x)
    parts = [hi, lo, hi]
    pad = -3 * x.shape[0] % LANES
    if pad:
        parts.append(jnp.zeros((pad, x.shape[1]), f32))
    return jnp.concatenate(parts, axis=0).astype(bf16)


def mm(a, b):
    return jnp.dot(a, b, preferred_element_type=f32)


def apply_l(x, jac, ld, dj, width):
    part = [x[:, q * width:(q + 1) * width] for q in range(NQ)]
    damp = jac[18:19]
    d_press = mm(ld, split3(part[0]))
    mixed = []
    for r in range(3):
        w = jac[3 * r:3 * r + 1] * part[1]
        for d in range(1, 3):
            w = w + jac[3 * r + d:3 * r + d + 1] * part[1 + d]
        mixed.append(split3(w))
    diverg = mm(dj, jnp.concatenate(mixed, axis=0))[:BR]
    rates = [diverg - damp * part[0]]
    for d in range(3):
        g = jac[9 + d:10 + d] * d_press[:BR]
        for r in range(1, 3):
            g = g + jac[9 + 3 * r + d:10 + 3 * r + d] * d_press[r * BR:(r + 1) * BR]
        rates.append(g - damp * part[1 + d])
    return jnp.concatenate(rates, axis=1)


def combine(terms, start_time, end_time):
    total = None
    for w, t in zip(weights(start_time, end_time), terms):
        total = w * t if total is None else total + w * t
    return total


def traces(x, pf, width):
    t = mm(pf, split3(x))
    cols = []
    for f in range(4):
        rows = [t[f * KR:(f + 1) * KR, q * width:(q + 1) * width] for q in range(NQ)]
        cols.append(jnp.concatenate(rows, axis=0))
    return cols


def gather(x, onehot):
    hi, lo = hi_lo(x)
    out = mm(jnp.concatenate([hi, lo], axis=0).astype(bf16), onehot)
    n = x.shape[0]
    return out[:n] + out[n:]


def lift(jumps, coef, lf, width, stride):
    flux = [[] for _ in range(NQ)]
    for f in range(4):
        c = coef[:, f * stride:f * stride + width]
        jp = jumps[f][:KR]
        ju = [jumps[f][(1 + d) * KR:(2 + d) * KR] for d in range(3)]
        lam = c[6:7]
        g = c[0:1] * ju[0]
        for d in range(1, 3):
            g = g + c[d:d + 1] * ju[d]
        flux[0].append(g - lam * jp)
        for d in range(3):
            flux[1 + d].append(c[3 + d:4 + d] * jp - lam * ju[d])
    cat = jnp.concatenate([jnp.concatenate(fl, axis=0) for fl in flux], axis=1)
    return mm(lf, split3(cat))[:BR]


def send_parts(sent, sub_id):
    sub = sent[:, 2 * LANES:]
    lane = lax.broadcasted_iota(jnp.int32, sub.shape, 1) // 32
    mine = lane == sub_id
    even = sub_id % 2 == 0
    r32 = pltpu.roll(sub, 32, 1)
    r96 = pltpu.roll(sub, 96, 1)
    zero = jnp.zeros_like(sub)
    return (
        sent[:, :LANES],
        sent[:, LANES:2 * LANES],
        jnp.where(mine, jnp.where(even, r96, r32), zero),
        jnp.where(mine, pltpu.roll(sub, 64, 1), zero),
        jnp.where(mine, jnp.where(even, r32, r96), zero),
        jnp.where(mine, sub, zero),
    )


def write_parts(refs, sent, sub_id):
    for ref, part in zip(refs, send_parts(sent, sub_id)):
        ref[...] = part


def received(refs, dom_id, n_dom):
    a, w, s1, s2, s3, own = [r[...] for r in refs]
    inner = jnp.logical_and(dom_id > 0, dom_id < n_dom - 1)
    w = jnp.where(inner, w, jnp.zeros_like(w))
    return jnp.concatenate([a, w, (s1 + s2) + (s3 + own)], axis=1)


def first_kernel(n_elem,
                 ids, start, inv_jac, normals, bulk, density, deriv, proj, liftm, cluster, pml,
                 dom_send, sub_send,
                 o_ld, o_dj, o_pf, o_lf, o_coef, o_jac, o_soh, o_x, o_p0, o_c1, o_c2, o_cs,
                 o_t0, m_a, m_w, m_1, m_2, m_3, m_own,
                 pad, lists):
    dom_id, sub_id = ids[0], ids[1]
    pad[...] = jnp.zeros_like(pad)
    for r in range(3):
        pad[r * BR:r * BR + NB, :NB] = deriv[r]
    hi, lo = hi_lo(pad[:3 * BR])
    left = hi + pltpu.roll(hi, BR, 1) + pltpu.roll(lo, 2 * BR, 1)
    zero8 = jnp.zeros((8, LANES), f32)
    ld = jnp.concatenate([left, zero8], axis=0).astype(bf16)
    dj = jnp.concatenate(
        [jnp.concatenate([left[r * BR:(r + 1) * BR], zero8], axis=0) for r in range(3)], axis=1
    ).astype(bf16)
    pad[...] = jnp.zeros_like(pad)
    for f in range(4):
        pad[f * KR:f * KR + NF, :NB] = proj[f]
    hi, lo = hi_lo(pad[:4 * KR])
    pf = (hi + pltpu.roll(hi, BR, 1) + pltpu.roll(lo, 2 * BR, 1)).astype(bf16)
    pad[...] = jnp.zeros_like(pad)
    for f in range(4):
        pad[f * 48:f * 48 + NB, :NF] = liftm[f]
    full = pad[:48]
    for f in range(1, 4):
        full = full + pltpu.roll(pad[f * 48:(f + 1) * 48], f * KR, 1)
    hi, lo = hi_lo(full)
    lf = jnp.concatenate([hi + pltpu.roll(hi, 64, 1), lo], axis=1).astype(bf16)
    o_ld[...] = ld
    o_dj[...] = dj
    o_pf[...] = pf
    o_lf[...] = lf
    bulk_row = bulk[...].reshape(1, n_elem)
    dens_row = density[...].reshape(1, n_elem)
    fine = jnp.where(cluster[...].reshape(1, n_elem) == 1, 1.0, 0.0).astype(f32)
    damp = sigma_pml * pml[...].reshape(1, n_elem).astype(f32)
    jac_in = inv_jac[...]
    o_jac[0:9] = -bulk_row * jac_in
    o_jac[9:18] = -jac_in / dens_row
    o_jac[18:19] = damp
    o_jac[19:20] = fine
    o_jac[20:24] = jnp.zeros((4, n_elem), f32)
    speed = jnp.sqrt(bulk_row / dens_row)
    for f in range(4):
        n = normals[3 * f:3 * f + 3]
        lanes = pl.ds(f * n_elem, n_elem)
        o_coef[0:3, lanes] = 0.5 * bulk_row * n
        o_coef[3:6, lanes] = 0.5 * n / dens_row
        o_coef[6:7, lanes] = 0.5 * speed * jnp.sqrt(jnp.sum(n * n, axis=0, keepdims=True))
        o_coef[7:8, lanes] = jnp.zeros((1, n_elem), f32)
    o_x[...] = jnp.zeros_like(o_x)
    for q in range(NQ):
        o_x[:NB, q * n_elem:(q + 1) * n_elem] = start[q * NB:(q + 1) * NB]
    x = o_x[...]
    jac = o_jac[...]
    terms = [x]
    for _ in range(ORDER - 1):
        terms.append(apply_l(terms[-1], jac, ld, dj, n_elem))
    p0 = combine(terms, 0.0, SUB_DT)
    o_p0[...] = p0
    o_c1[...] = combine(terms, SUB_DT, 2 * SUB_DT)
    o_c2[...] = combine(terms, 2 * SUB_DT, 3 * SUB_DT)
    o_cs[...] = combine(terms, 0.0, step_size)
    t0 = jnp.concatenate(traces(p0, pf, n_elem), axis=1)
    o_t0[...] = t0
    lists[...] = jnp.full(lists.shape, -1, jnp.int32)
    even = dom_id % 2 == 0
    before, after = dom_send[0:1], dom_send[1:2]
    n_halo = before.shape[1]
    lists[0:1, :n_halo] = jnp.where(even, after, before)
    lists[0:1, LANES:LANES + n_halo] = jnp.where(even, before, after)
    for b in range(4):
        lists[0:1, 2 * LANES + 32 * b:2 * LANES + 32 * (b + 1)] = sub_send[b:b + 1]
    names = lists[0:1]
    n_face = 4 * n_elem
    step = 256
    for j in range(0, n_face, step):
        row = j + lax.broadcasted_iota(jnp.int32, (step, 3 * LANES), 0)
        o_soh[j:j + step] = jnp.where(row == names, 1.0, 0.0).astype(bf16)
    write_parts((m_a, m_w, m_1, m_2, m_3, m_own), gather(t0, o_soh[...]), sub_id)


def fine_base(state, pub, t, roh, coef, jac, ld, dj, lf, n_elem):
    tile = LANES
    jumps = []
    for f in range(4):
        own = t[:, f * n_elem:f * n_elem + tile]
        got = gather(t, roh[:4 * n_elem, f * n_elem:f * n_elem + tile])
        jumps.append(got - own)
    corr = lift(jumps, coef, lf, tile, n_elem)
    return state + apply_l(pub, jac, ld, dj, tile) - corr


def head(x, n_elem):
    return jnp.concatenate(
        [x[:, q * n_elem:q * n_elem + LANES] for q in range(NQ)], axis=1
    )


def table_kernel(n_elem, n_halo, ids, neighbours, roh):
    dom_id = ids[0]
    n_face = 4 * n_elem
    even = dom_id % 2 == 0
    nbr = neighbours[...]
    before_at = jnp.where(even, n_face + LANES, n_face)
    after_at = jnp.where(even, n_face, n_face + LANES)
    at = jnp.where(
        nbr < n_face,
        nbr,
        jnp.where(
            nbr < n_face + n_halo,
            nbr - n_face + before_at,
            jnp.where(
                nbr < n_face + 2 * n_halo,
                nbr - (n_face + n_halo) + after_at,
                nbr - (n_face + 2 * n_halo) + n_face + 2 * LANES,
            ),
        ),
    )
    step = 128
    for f in range(4):
        col = at[f:f + 1]
        for j in range(0, n_face + 3 * LANES, step):
            row = j + lax.broadcasted_iota(jnp.int32, (step, n_elem), 0)
            roh[j:j + step, f * n_elem:(f + 1) * n_elem] = jnp.where(row == col, 1.0, 0.0).astype(bf16)


def window0_kernel(n_elem, x, p0, c1, c2, cs, t0, roh, soh, coef, jac, ld, dj, pf, lf,
                   o_base, o_t1, o_t2, o_ts, o_s1, o_s2, o_ss):
    jac_h = jac[:, :LANES]
    o_base[...] = fine_base(head(x[...], n_elem), head(p0[...], n_elem), t0[...], roh, coef[...],
                            jac_h, ld[...], dj[...], lf[...], n_elem)
    fine = jac[19:20]
    fine4 = jnp.concatenate([fine] * 4, axis=1)
    for c, o_t, o_s in ((c1, o_t1, o_s1), (c2, o_t2, o_s2), (cs, o_ts, o_ss)):
        t = jnp.concatenate(traces(c[...], pf[...], n_elem), axis=1)
        t = jnp.where(fine4 > 0.5, 0.0, t)
        o_t[...] = t
        o_s[...] = gather(t, soh[...])


def step_kernel(n_elem, n_dom, last,
                ids, r_a, r_w, r_1, r_2, r_3, r_own, base, p_sum, t_coarse, s_coarse,
                roh, soh, coef, jac, ld, dj, pf, lf,
                o_state, o_pub, o_sum, o_t, m_a, m_w, m_1, m_2, m_3, m_own):
    dom_id, sub_id = ids[0], ids[1]
    n_face = 4 * n_elem
    tile = LANES
    got = received((r_a, r_w, r_1, r_2, r_3, r_own), dom_id, n_dom)
    jumps = [gather(got, roh[n_face:, f * n_elem:f * n_elem + tile]) for f in range(4)]
    state = base[...] - lift(jumps, coef[...], lf[...], tile, n_elem)
    jac_h = jac[:, :tile]
    terms = [state]
    for _ in range(ORDER - 1):
        terms.append(apply_l(terms[-1], jac_h, ld[...], dj[...], tile))
    pub = combine(terms, 0.0, SUB_DT)
    total = p_sum[...] + pub
    o_state[...] = state
    o_pub[...] = pub
    o_sum[...] = total
    fine = jac_h[19:20] > 0.5
    zero = jnp.zeros((4 * KR, tile), f32)
    fine_t = [jnp.where(fine, t, zero) for t in traces(total if last else pub, pf[...], tile)]
    o_t[...] = t_coarse[...]
    for f in range(4):
        o_t[:, f * n_elem:f * n_elem + tile] += fine_t[f]
    sent = s_coarse[...]
    for f in range(4):
        sent = sent + gather(fine_t[f], soh[f * n_elem:f * n_elem + tile])
    write_parts((m_a, m_w, m_1, m_2, m_3, m_own), sent, sub_id)


def window_kernel(n_elem, state, pub, t, roh, coef, jac, ld, dj, lf, o_base):
    o_base[...] = fine_base(state[...], pub[...], t[...], roh, coef[...], jac[:, :LANES], ld[...],
                            dj[...], lf[...], n_elem)


def window3_kernel(n_elem, x, cs, total, t, roh, coef, jac, ld, dj, lf, o_base):
    fine = jac[19:20, :LANES] > 0.5
    parts = []
    for q in range(NQ):
        c = cs[:, q * n_elem:(q + 1) * n_elem]
        parts.append(jnp.where(fine, total[:, q * LANES:(q + 1) * LANES], c[:, :LANES]))
        parts.append(c[:, LANES:])
    pub = jnp.concatenate(parts, axis=1)
    tv = t[...]
    jumps = []
    for f in range(4):
        lanes = slice(f * n_elem, (f + 1) * n_elem)
        jumps.append(gather(tv, roh[:4 * n_elem, lanes]) - tv[:, lanes])
    corr = lift(jumps, coef[...], lf[...], n_elem, n_elem)
    o_base[...] = x[...] + apply_l(pub, jac[...], ld[...], dj[...], n_elem) - corr


def last_kernel(n_elem, n_dom, ids, r_a, r_w, r_1, r_2, r_3, r_own, base, roh, coef, lf, out):
    n_face = 4 * n_elem
    got = received((r_a, r_w, r_1, r_2, r_3, r_own), ids[0], n_dom)
    jumps = [gather(got, roh[n_face:, f * n_elem:(f + 1) * n_elem]) for f in range(4)]
    res = base[...] - lift(jumps, coef[...], lf[...], n_elem, n_elem)
    for q in range(NQ):
        out[q * NB:(q + 1) * NB] = res[:NB, q * n_elem:(q + 1) * n_elem]


def call(kernel, name, outs, args, scratch=(), raw=(), hbm_out=False, flops=0):
    vm = pl.BlockSpec(memory_space=pltpu.VMEM)
    sm = pl.BlockSpec(memory_space=pltpu.SMEM)
    specs, ops = [], []
    for i, a in enumerate(args):
        if a.ndim == 1 and a.shape[0] == 2:
            specs.append(sm)
            ops.append(a)
        elif i in raw:
            specs.append(vm)
            ops.append(a)
        else:
            specs.append(vm)
            ops.append(pltpu.with_memory_space_constraint(a, pltpu.VMEM))
    shapes = [
        jax.ShapeDtypeStruct(s, d) if hbm_out else pltpu.VMEM(s, d) for s, d in outs
    ]
    return pl.pallas_call(
        kernel,
        in_specs=specs,
        out_specs=[vm] * len(shapes),
        out_shape=shapes,
        scratch_shapes=list(scratch),
        name=name,
        compiler_params=pltpu.CompilerParams(vmem_limit_bytes=16 << 20),
        cost_estimate=pl.CostEstimate(flops=flops, bytes_accessed=1 << 16, transcendentals=0),
    )(*ops)


def exchange(parts, n_dom):
    a, w, s1, s2, s3, own = parts
    other = [(i, ((i + 1) ^ 1) - 1 if 0 < i < n_dom - 1 else n_dom - 1 - i) for i in range(n_dom)]
    r1 = lax.ppermute(s1, "sub", [(i, i ^ 1) for i in range(4)])
    ra = lax.ppermute(a, "dom", [(i, i ^ 1) for i in range(n_dom)])
    r3 = lax.ppermute(s3, "sub", [(i, i ^ 3) for i in range(4)])
    rw = lax.ppermute(w, "dom", other)
    r2 = lax.ppermute(s2, "sub", [(i, i ^ 2) for i in range(4)])
    return ra, rw, r1, r2, r3, own


def make_body(n_dom, n_sub):
    assert n_dom % 2 == 0 and n_sub == 4

    def body(start_dofs, inv_jac, normals, bulk_modulus, density, deriv_mats, face_proj, face_lift,
             cluster, pml_flags, neighbours, dom_send, sub_send):
        n_elem = start_dofs.shape[1]
        n_halo = dom_send.shape[1]
        n_face = 4 * n_elem
        ids = jnp.stack([lax.axis_index("dom"), lax.axis_index("sub")]).astype(jnp.int32)
        wide = ((BR, NQ * n_elem), f32)
        slim = ((BR, NQ * LANES), f32)
        trace = ((4 * KR, n_face), f32)
        listed = ((4 * KR, 3 * LANES), f32)
        msg = ((4 * KR, LANES), f32)
        first = call(
            lambda *r: first_kernel(n_elem, *r), "first",
            [((128, 128), bf16), ((48, 384), bf16), ((64, 128), bf16), ((48, 256), bf16),
             ((8, n_face), f32), ((24, n_elem), f32), ((n_face, 3 * LANES), bf16)]
            + [wide] * 5 + [trace] + [msg] * 6,
            [ids, start_dofs, inv_jac, normals, bulk_modulus, density, deriv_mats, face_proj,
             face_lift, cluster, pml_flags, dom_send, sub_send],
            raw=range(13),
            scratch=[pltpu.VMEM((192, LANES), f32), pltpu.VMEM((8, 3 * LANES), jnp.int32)],
        )
        ld, dj, pf, lf, coef, jac, soh, x, p0, c1, c2, cs, t0 = first[:13]
        (roh,) = call(
            lambda *r: table_kernel(n_elem, n_halo, *r), "table",
            [((n_face + 3 * LANES, n_face), bf16)], [ids, neighbours], raw=(1,), flops=1 << 28,
        )
        got = exchange(first[13:], n_dom)
        base, t1, t2, ts, s1, s2, ss = call(
            lambda *r: window0_kernel(n_elem, *r), "window0",
            [slim] + [trace] * 3 + [listed] * 3,
            [x, p0, c1, c2, cs, t0, roh, soh, coef, jac, ld, dj, pf, lf], flops=1 << 29,
        )
        total = jnp.concatenate(
            [p0[:, q * n_elem:q * n_elem + LANES] for q in range(NQ)], axis=1
        )
        for s, (t_c, s_c) in enumerate(((t1, s1), (t2, s2), (ts, ss))):
            last = s == 2
            outs = call(
                lambda *r, last=last: step_kernel(n_elem, n_dom, last, *r), "step",
                [slim] * 3 + [trace] + [msg] * 6,
                [ids, *got, base, total, t_c, s_c, roh, soh, coef, jac, ld, dj, pf, lf],
            )
            state, pub, total, t = outs[:4]
            got = exchange(outs[4:], n_dom)
            if last:
                (base,) = call(
                    lambda *r: window3_kernel(n_elem, *r), "window3", [wide],
                    [x, cs, total, t, roh, coef, jac, ld, dj, lf], flops=1 << 29,
                )
            else:
                (base,) = call(
                    lambda *r: window_kernel(n_elem, *r), "window", [slim],
                    [state, pub, t, roh, coef, jac, ld, dj, lf], flops=1 << 28,
                )
        (out,) = call(
            lambda *r: last_kernel(n_elem, n_dom, *r), "last",
            [((NQ * NB, n_elem), f32)], [ids, *got, base, roh, coef, lf], hbm_out=True,
        )
        return out

    return body


def solution(mesh):
    in_specs = (
        P(None, ("dom", "sub")),
        P(None, ("dom", "sub")),
        P(None, ("dom", "sub")),
        P(("dom", "sub")),
        P(("dom", "sub")),
        P(),
        P(),
        P(),
        P(("dom", "sub")),
        P(("dom", "sub")),
        P(None, ("dom", "sub")),
        P(("dom", "sub"), None),
        P(("dom", "sub"), None),
    )
    out_specs = P(None, ("dom", "sub"))
    body = make_body(mesh.shape["dom"], mesh.shape["sub"])
    return jax.shard_map(body, mesh=mesh, in_specs=in_specs, out_specs=out_specs, check_vma=False)
```

```python
import math

import jax
import jax.numpy as jnp
from jax import lax
from jax.experimental import pallas as pl
from jax.experimental.pallas import tpu as pltpu
from jax.sharding import PartitionSpec as P

NQ = 4
NB = 35
NF = 15
ORDER = 5
SUBSTEPS = 4
BR = 40
KR = 16
LANES = 128

step_size = 0.8
sigma_pml = 1.5
f32 = jnp.float32
bf16 = jnp.bfloat16


def weights(start_time, end_time):
    return [
        (end_time ** (k + 1) - start_time ** (k + 1)) / math.factorial(k + 1)
        for k in range(ORDER)
    ]


SUB_DT = step_size / SUBSTEPS


def hi_lo(x):
    hi = x.astype(bf16).astype(f32)
    return hi, x - hi


def split3(x):
    hi, lo = hi_lo(x)
    parts = [hi, lo, hi]
    pad = -3 * x.shape[0] % LANES
    if pad:
        parts.append(jnp.zeros((pad, x.shape[1]), f32))
    return jnp.concatenate(parts, axis=0).astype(bf16)


def mm(a, b):
    return jnp.dot(a, b, preferred_element_type=f32)


def apply_l(x, jac, ld, dj, width):
    part = [x[:, q * width:(q + 1) * width] for q in range(NQ)]
    damp = jac[18:19]
    d_press = mm(ld, split3(part[0]))
    mixed = []
    for r in range(3):
        w = jac[3 * r:3 * r + 1] * part[1]
        for d in range(1, 3):
            w = w + jac[3 * r + d:3 * r + d + 1] * part[1 + d]
        mixed.append(split3(w))
    diverg = mm(dj, jnp.concatenate(mixed, axis=0))[:BR]
    rates = [diverg - damp * part[0]]
    for d in range(3):
        g = jac[9 + d:10 + d] * d_press[:BR]
        for r in range(1, 3):
            g = g + jac[9 + 3 * r + d:10 + 3 * r + d] * d_press[r * BR:(r + 1) * BR]
        rates.append(g - damp * part[1 + d])
    return jnp.concatenate(rates, axis=1)


def combine(terms, start_time, end_time):
    total = None
    for w, t in zip(weights(start_time, end_time), terms):
        total = w * t if total is None else total + w * t
    return total


def traces(x, pf, width):
    t = mm(pf, split3(x))
    cols = []
    for f in range(4):
        rows = [t[f * KR:(f + 1) * KR, q * width:(q + 1) * width] for q in range(NQ)]
        cols.append(jnp.concatenate(rows, axis=0))
    return cols


def gather(x, onehot):
    hi, lo = hi_lo(x)
    out = mm(jnp.concatenate([hi, lo], axis=0).astype(bf16), onehot)
    n = x.shape[0]
    return out[:n] + out[n:]


def lift(jumps, coef, lf, width, stride):
    flux = [[] for _ in range(NQ)]
    for f in range(4):
        c = coef[:, f * stride:f * stride + width]
        jp = jumps[f][:KR]
        ju = [jumps[f][(1 + d) * KR:(2 + d) * KR] for d in range(3)]
        lam = c[6:7]
        g = c[0:1] * ju[0]
        for d in range(1, 3):
            g = g + c[d:d + 1] * ju[d]
        flux[0].append(g - lam * jp)
        for d in range(3):
            flux[1 + d].append(c[3 + d:4 + d] * jp - lam * ju[d])
    cat = jnp.concatenate([jnp.concatenate(fl, axis=0) for fl in flux], axis=1)
    return mm(lf, split3(cat))[:BR]


def block_mask(shape, block):
    return lax.broadcasted_iota(jnp.int32, shape, 1) // 32 == block


def turn(x, blocks):
    blocks %= 4
    return pltpu.roll(x, 32 * blocks, 1) if blocks else x


def write_parts(refs, sent):
    m_a, m_w, m_1, m_2, m_3, m_own = refs
    m_a[...] = sent[:, :LANES]
    m_w[...] = sent[:, LANES:2 * LANES]
    sub = sent[:, 2 * LANES:]
    for k, ref in ((1, m_1), (2, m_2), (3, m_3)):
        msg = turn(sub[:KR], -k)
        for q in range(1, NQ):
            msg = jnp.where(block_mask(msg.shape, q), turn(sub[q * KR:(q + 1) * KR], q - k), msg)
        ref[...] = msg
    m_own[...] = sub


def received(refs, dom_id, n_dom):
    a, w, s1, s2, s3 = [refs[TAKEN.index(i)][...] for i in range(5)]
    own = refs[5][...]
    inner = jnp.logical_and(dom_id > 0, dom_id < n_dom - 1)
    w = jnp.where(inner, w, jnp.zeros_like(w))
    rows = []
    for q in range(NQ):
        row = own[q * KR:(q + 1) * KR]
        for k, msg in ((1, s1), (2, s2), (3, s3)):
            row = jnp.where(block_mask(row.shape, k), turn(msg, k - q), row)
        rows.append(row)
    return jnp.concatenate([a, w, jnp.concatenate(rows, axis=0)], axis=1)


def first_kernel(n_elem, *refs):
    ids, raw = refs[0], refs[1:14]
    (o_ld, o_dj, o_pf, o_lf, o_coef, o_jac, o_soh, o_at, o_x, o_xh, o_ph, o_c1, o_c2, o_cs,
     o_t0, m_a, m_w, m_1, m_2, m_3, m_own) = refs[14:35]
    held, sem, pad, lists = refs[35:48], refs[48], refs[49], refs[50]
    copies = [
        pltpu.make_async_copy(src, dst, sem.at[i]) for i, (src, dst) in enumerate(zip(raw, held))
    ]
    for c in copies:
        c.start()
    (start, inv_jac, normals, bulk, density, deriv, proj, liftm, cluster, pml, neighbours,
     dom_send, sub_send) = held
    pad[...] = jnp.zeros_like(pad)
    o_x[...] = jnp.zeros_like(o_x)
    for c in copies:
        c.wait()
    dom_id, sub_id = ids[0], ids[1]
    for r in range(3):
        pad[r * BR:r * BR + NB, :NB] = deriv[r]
    hi, lo = hi_lo(pad[:3 * BR])
    left = hi + pltpu.roll(hi, BR, 1) + pltpu.roll(lo, 2 * BR, 1)
    zero8 = jnp.zeros((8, LANES), f32)
    ld = jnp.concatenate([left, zero8], axis=0).astype(bf16)
    dj = jnp.concatenate(
        [jnp.concatenate([left[r * BR:(r + 1) * BR], zero8], axis=0) for r in range(3)], axis=1
    ).astype(bf16)
    pad[...] = jnp.zeros_like(pad)
    for f in range(4):
        pad[f * KR:f * KR + NF, :NB] = proj[:, f, :]
    hi, lo = hi_lo(pad[:4 * KR])
    pf = (hi + pltpu.roll(hi, BR, 1) + pltpu.roll(lo, 2 * BR, 1)).astype(bf16)
    pad[...] = jnp.zeros_like(pad)
    for f in range(4):
        pad[f * KR:f * KR + NF, :NB] = liftm[:, f, :]
    full = jnp.transpose(pad[:LANES])[:48]
    hi, lo = hi_lo(full)
    lf = jnp.concatenate([hi + pltpu.roll(hi, 64, 1), lo], axis=1).astype(bf16)
    o_ld[...] = ld
    o_dj[...] = dj
    o_pf[...] = pf
    o_lf[...] = lf
    bulk_row = bulk[...].reshape(1, n_elem)
    dens_row = density[...].reshape(1, n_elem)
    fine = jnp.where(cluster[...].reshape(1, n_elem) == 1, 1.0, 0.0).astype(f32)
    damp = sigma_pml * pml[...].reshape(1, n_elem).astype(f32)
    jac_in = inv_jac[...]
    o_jac[0:9] = -bulk_row * jac_in
    o_jac[9:18] = -jac_in / dens_row
    o_jac[18:19] = damp
    o_jac[19:20] = fine
    o_jac[20:24] = jnp.zeros((4, n_elem), f32)
    speed = jnp.sqrt(bulk_row / dens_row)
    for f in range(4):
        n = normals[3 * f:3 * f + 3]
        lanes = pl.ds(f * n_elem, n_elem)
        o_coef[0:3, lanes] = 0.5 * bulk_row * n
        o_coef[3:6, lanes] = 0.5 * n / dens_row
        o_coef[6:7, lanes] = 0.5 * speed * jnp.sqrt(jnp.sum(n * n, axis=0, keepdims=True))
        o_coef[7:8, lanes] = jnp.zeros((1, n_elem), f32)
    for q in range(NQ):
        o_x[:NB, q * n_elem:(q + 1) * n_elem] = start[q * NB:(q + 1) * NB]
    x = o_x[...]
    jac = o_jac[...]
    terms = [x]
    for _ in range(ORDER - 1):
        terms.append(apply_l(terms[-1], jac, ld, dj, n_elem))
    p0 = combine(terms, 0.0, SUB_DT)
    o_xh[...] = head(x, n_elem)
    o_ph[...] = head(p0, n_elem)
    o_c1[...] = combine(terms, SUB_DT, 2 * SUB_DT)
    o_c2[...] = combine(terms, 2 * SUB_DT, 3 * SUB_DT)
    o_cs[...] = combine(terms, 0.0, step_size)
    t0 = jnp.concatenate(traces(p0, pf, n_elem), axis=1)
    o_t0[...] = t0
    lists[...] = jnp.full(lists.shape, -1, jnp.int32)
    even = dom_id % 2 == 0
    before, after = dom_send[0:1], dom_send[1:2]
    n_halo = before.shape[1]
    lists[0:1, :n_halo] = jnp.where(even, after, before)
    lists[0:1, LANES:LANES + n_halo] = jnp.where(even, before, after)
    for b in range(4):
        lists[0:1, 2 * LANES + 32 * b:2 * LANES + 32 * (b + 1)] = sub_send[pl.ds(sub_id ^ b, 1)]
    names = lists[0:1]
    n_face = 4 * n_elem
    step = 256
    for j in range(0, n_face, step):
        row = j + lax.broadcasted_iota(jnp.int32, (step, 3 * LANES), 0)
        o_soh[j:j + step] = jnp.where(row == names, 1.0, 0.0).astype(bf16)
    write_parts((m_a, m_w, m_1, m_2, m_3, m_own), gather(t0, o_soh[...]))
    nbr = neighbours[...]
    before_at = jnp.where(even, n_face + LANES, n_face)
    after_at = jnp.where(even, n_face, n_face + LANES)
    slot = nbr - (n_face + 2 * n_halo)
    o_at[...] = jnp.where(
        nbr < n_face,
        nbr,
        jnp.where(
            nbr < n_face + n_halo,
            nbr - n_face + before_at,
            jnp.where(
                nbr < n_face + 2 * n_halo,
                nbr - (n_face + n_halo) + after_at,
                n_face + 2 * LANES + 32 * ((slot >> 5) ^ sub_id) + (slot & 31),
            ),
        ),
    )


def fine_base(state, pub, t, roh, coef, jac, ld, dj, lf, n_elem):
    tile = LANES
    jumps = []
    for f in range(4):
        own = t[:, f * n_elem:f * n_elem + tile]
        got = gather(t, roh[:4 * n_elem, f * tile:(f + 1) * tile])
        jumps.append(got - own)
    corr = lift(jumps, coef, lf, tile, n_elem)
    return state + apply_l(pub, jac, ld, dj, tile) - corr


def head(x, n_elem):
    return jnp.concatenate(
        [x[:, q * n_elem:q * n_elem + LANES] for q in range(NQ)], axis=1
    )


def table(at, roh, n_elem, first, count):
    step = 128
    for f in range(4):
        col = at[f:f + 1, first:first + count]
        for j in range(0, roh.shape[0], step):
            row = j + lax.broadcasted_iota(jnp.int32, (step, count), 0)
            roh[j:j + step, f * count:(f + 1) * count] = jnp.where(row == col, 1.0, 0.0).astype(bf16)


def coarse_traces(c, soh, jac, pf, o_t, o_s, n_elem):
    fine4 = jnp.concatenate([jac[19:20]] * 4, axis=1)
    t = jnp.concatenate(traces(c[...], pf[...], n_elem), axis=1)
    t = jnp.where(fine4 > 0.5, 0.0, t)
    o_t[...] = t
    o_s[...] = gather(t, soh[...])


def window0_kernel(n_elem, at, xh, ph, c1, t0, soh, coef, jac, ld, dj, pf, lf,
                   roh, o_base, o_t1, o_s1):
    table(at, roh, n_elem, 0, LANES)
    o_base[...] = fine_base(xh[...], ph[...], t0[...], roh, coef[...], jac[:, :LANES], ld[...],
                            dj[...], lf[...], n_elem)
    coarse_traces(c1, soh, jac, pf, o_t1, o_s1, n_elem)


def step_kernel(n_elem, n_dom, last,
                ids, r_a, r_w, r_1, r_2, r_3, r_own, base, p_sum, t_coarse, s_coarse,
                roh, soh, coef, jac, ld, dj, pf, lf,
                o_state, o_pub, o_sum, o_t, m_a, m_w, m_1, m_2, m_3, m_own):
    n_face = 4 * n_elem
    tile = LANES
    got = received((r_a, r_w, r_1, r_2, r_3, r_own), ids[0], n_dom)
    jumps = [gather(got, roh[n_face:, f * tile:(f + 1) * tile]) for f in range(4)]
    state = base[...] - lift(jumps, coef[...], lf[...], tile, n_elem)
    jac_h = jac[:, :tile]
    terms = [state]
    for _ in range(ORDER - 1):
        terms.append(apply_l(terms[-1], jac_h, ld[...], dj[...], tile))
    pub = combine(terms, 0.0, SUB_DT)
    total = p_sum[...] + pub
    o_state[...] = state
    o_pub[...] = pub
    o_sum[...] = total
    fine = jac_h[19:20] > 0.5
    zero = jnp.zeros((4 * KR, tile), f32)
    fine_t = [jnp.where(fine, t, zero) for t in traces(total if last else pub, pf[...], tile)]
    o_t[...] = t_coarse[...]
    for f in range(4):
        o_t[:, f * n_elem:f * n_elem + tile] += fine_t[f]
    sent = s_coarse[...]
    for f in range(4):
        sent = sent + gather(fine_t[f], soh[f * n_elem:f * n_elem + tile])
    write_parts((m_a, m_w, m_1, m_2, m_3, m_own), sent)


def window_kernel(n_elem, tabled, at, state, pub, t, c, roh, soh, coef, jac, ld, dj, pf, lf,
                  o_base, o_t, o_s, *o_roh):
    o_base[...] = fine_base(state[...], pub[...], t[...], roh, coef[...], jac[:, :LANES], ld[...],
                            dj[...], lf[...], n_elem)
    coarse_traces(c, soh, jac, pf, o_t, o_s, n_elem)
    if tabled:
        table(at, o_roh[0], n_elem, LANES, n_elem - LANES)


def split_gather(x, roh, roh2, rows, f, n_elem):
    rest = n_elem - LANES
    return jnp.concatenate(
        [gather(x, roh[rows, f * LANES:(f + 1) * LANES]), gather(x, roh2[rows, f * rest:(f + 1) * rest])],
        axis=1,
    )


def window3_kernel(n_elem, x, cs, total, t, roh, roh2, coef, jac, ld, dj, lf, o_base):
    fine = jac[19:20, :LANES] > 0.5
    parts = []
    for q in range(NQ):
        c = cs[:, q * n_elem:(q + 1) * n_elem]
        parts.append(jnp.where(fine, total[:, q * LANES:(q + 1) * LANES], c[:, :LANES]))
        parts.append(c[:, LANES:])
    pub = jnp.concatenate(parts, axis=1)
    tv = t[...]
    rows = slice(0, 4 * n_elem)
    jumps = [
        split_gather(tv, roh, roh2, rows, f, n_elem) - tv[:, f * n_elem:(f + 1) * n_elem]
        for f in range(4)
    ]
    corr = lift(jumps, coef[...], lf[...], n_elem, n_elem)
    o_base[...] = x[...] + apply_l(pub, jac[...], ld[...], dj[...], n_elem) - corr


def last_kernel(n_elem, n_dom, ids, r_a, r_w, r_1, r_2, r_3, r_own, base, roh, roh2, coef, lf, out):
    got = received((r_a, r_w, r_1, r_2, r_3, r_own), ids[0], n_dom)
    rows = slice(4 * n_elem, 4 * n_elem + 3 * LANES)
    jumps = [split_gather(got, roh, roh2, rows, f, n_elem) for f in range(4)]
    res = base[...] - lift(jumps, coef[...], lf[...], n_elem, n_elem)
    for q in range(NQ):
        out[q * NB:(q + 1) * NB] = res[:NB, q * n_elem:(q + 1) * n_elem]


def call(kernel, name, outs, args, scratch=(), raw=(), hbm_out=False, flops=0):
    vm = pl.BlockSpec(memory_space=pltpu.VMEM)
    sm = pl.BlockSpec(memory_space=pltpu.SMEM)
    specs, ops = [], []
    for i, a in enumerate(args):
        if a.ndim == 1 and a.shape[0] == 2:
            specs.append(sm)
            ops.append(a)
        elif i in raw:
            specs.append(pl.BlockSpec(memory_space=pltpu.HBM))
            ops.append(pltpu.with_memory_space_constraint(a, pltpu.HBM))
        else:
            specs.append(vm)
            ops.append(pltpu.with_memory_space_constraint(a, pltpu.VMEM))
    shapes = [
        jax.ShapeDtypeStruct(s, d) if hbm_out else pltpu.VMEM(s, d) for s, d in outs
    ]
    return pl.pallas_call(
        kernel,
        in_specs=specs,
        out_specs=[vm] * len(shapes),
        out_shape=shapes,
        scratch_shapes=list(scratch),
        name=name,
        compiler_params=pltpu.CompilerParams(vmem_limit_bytes=16 << 20),
        cost_estimate=pl.CostEstimate(flops=flops, bytes_accessed=1 << 16, transcendentals=0),
    )(*ops)


TAKEN = (4, 3, 2, 1, 0)


def exchange(parts, n_dom):
    a, w, s1, s2, s3, own = parts
    other = [(i, ((i + 1) ^ 1) - 1 if 0 < i < n_dom - 1 else n_dom - 1 - i) for i in range(n_dom)]
    r1 = lax.ppermute(s1, "sub", [(i, i ^ 1) for i in range(4)])
    ra = lax.ppermute(a, "dom", [(i, i ^ 1) for i in range(n_dom)])
    r3 = lax.ppermute(s3, "sub", [(i, i ^ 3) for i in range(4)])
    rw = lax.ppermute(w, "dom", other)
    r2 = lax.ppermute(s2, "sub", [(i, i ^ 2) for i in range(4)])
    got = (ra, rw, r1, r2, r3)
    return tuple(got[i] for i in TAKEN) + (own,)


def make_body(n_dom, n_sub):
    assert n_dom % 2 == 0 and n_sub == 4

    def body(start_dofs, inv_jac, normals, bulk_modulus, density, deriv_mats, face_proj, face_lift,
             cluster, pml_flags, neighbours, dom_send, sub_send):
        n_elem = start_dofs.shape[1]
        n_halo = dom_send.shape[1]
        n_face = 4 * n_elem
        ids = jnp.stack([lax.axis_index("dom"), lax.axis_index("sub")]).astype(jnp.int32)
        wide = ((BR, NQ * n_elem), f32)
        slim = ((BR, NQ * LANES), f32)
        trace = ((4 * KR, n_face), f32)
        listed = ((4 * KR, 3 * LANES), f32)
        msg = ((4 * KR, LANES), f32)
        small = ((KR, LANES), f32)
        msgs = [msg, msg, small, small, small, msg]
        half = ((n_face + 3 * LANES, 4 * LANES), bf16)
        rest = ((n_face + 3 * LANES, 4 * (n_elem - LANES)), bf16)
        raw = [start_dofs, inv_jac, normals, bulk_modulus, density, deriv_mats,
               jnp.transpose(face_proj, (1, 0, 2)), jnp.transpose(face_lift, (2, 0, 1)),
               cluster, pml_flags, neighbours, dom_send, sub_send]
        first = call(
            lambda *r: first_kernel(n_elem, *r), "first",
            [((128, 128), bf16), ((48, 384), bf16), ((64, 128), bf16), ((48, 256), bf16),
             ((8, n_face), f32), ((24, n_elem), f32), ((n_face, 3 * LANES), bf16),
             ((4, n_elem), jnp.int32), wide, slim, slim, wide, wide, wide, trace] + msgs,
            [ids] + raw, raw=range(1, 14),
            scratch=[pltpu.VMEM(a.shape, a.dtype) for a in raw]
            + [pltpu.SemaphoreType.DMA((len(raw),)), pltpu.VMEM((128, LANES), f32),
               pltpu.VMEM((8, 3 * LANES), jnp.int32)],
        )
        ld, dj, pf, lf, coef, jac, soh, at, x, xh, total, c1, c2, cs, t = first[:15]
        got = exchange(first[15:], n_dom)
        roh, base, t_c, s_c = call(
            lambda *r: window0_kernel(n_elem, *r), "window0", [half, slim, trace, listed],
            [at, xh, total, c1, t, soh, coef, jac, ld, dj, pf, lf], flops=1 << 28,
        )
        roh2 = None
        for s in range(SUBSTEPS - 1):
            last = s == SUBSTEPS - 2
            outs = call(
                lambda *r, last=last: step_kernel(n_elem, n_dom, last, *r), "step",
                [slim] * 3 + [trace] + msgs,
                [ids, *got, base, total, t_c, s_c, roh, soh, coef, jac, ld, dj, pf, lf],
            )
            state, pub, total, t = outs[:4]
            got = exchange(outs[4:], n_dom)
            if last:
                (base,) = call(
                    lambda *r: window3_kernel(n_elem, *r), "window3", [wide],
                    [x, cs, total, t, roh, roh2, coef, jac, ld, dj, lf], flops=1 << 28,
                )
            else:
                res = call(
                    lambda *r, s=s: window_kernel(n_elem, s == 0, *r), "window",
                    [slim, trace, listed] + ([rest] if s == 0 else []),
                    [at, state, pub, t, (c2, cs)[s], roh, soh, coef, jac, ld, dj, pf, lf],
                    flops=1 << 28,
                )
                base, t_c, s_c = res[:3]
                if s == 0:
                    roh2 = res[3]
        (out,) = call(
            lambda *r: last_kernel(n_elem, n_dom, *r), "last",
            [((NQ * NB, n_elem), f32)], [ids, *got, base, roh, roh2, coef, lf], hbm_out=True,
        )
        return out

    return body


def solution(mesh):
    in_specs = (
        P(None, ("dom", "sub")),
        P(None, ("dom", "sub")),
        P(None, ("dom", "sub")),
        P(("dom", "sub")),
        P(("dom", "sub")),
        P(),
        P(),
        P(),
        P(("dom", "sub")),
        P(("dom", "sub")),
        P(None, ("dom", "sub")),
        P(("dom", "sub"), None),
        P(("dom", "sub"), None),
    )
    out_specs = P(None, ("dom", "sub"))
    body = make_body(mesh.shape["dom"], mesh.shape["sub"])
    return jax.shard_map(body, mesh=mesh, in_specs=in_specs, out_specs=out_specs, check_vma=False)
```

```python
import math

import jax
import jax.numpy as jnp
from jax import lax
from jax.experimental import pallas as pl
from jax.experimental.pallas import tpu as pltpu
from jax.sharding import PartitionSpec as P

NQ = 4
NB = 35
NF = 15
ORDER = 5
SUBSTEPS = 4
BR = 40
KR = 16
LANES = 128

step_size = 0.8
sigma_pml = 1.5
f32 = jnp.float32
bf16 = jnp.bfloat16


def weights(start_time, end_time):
    return [
        (end_time ** (k + 1) - start_time ** (k + 1)) / math.factorial(k + 1)
        for k in range(ORDER)
    ]


SUB_DT = step_size / SUBSTEPS


def hi_lo(x):
    hi = x.astype(bf16).astype(f32)
    return hi, x - hi


def split3(x):
    hi, lo = hi_lo(x)
    parts = [hi, lo, hi]
    pad = -3 * x.shape[0] % LANES
    if pad:
        parts.append(jnp.zeros((pad, x.shape[1]), f32))
    return jnp.concatenate(parts, axis=0).astype(bf16)


def mm(a, b):
    return jnp.dot(a, b, preferred_element_type=f32)


def apply_l(x, jac, ld, dj, width):
    part = [x[:, q * width:(q + 1) * width] for q in range(NQ)]
    damp = jac[18:19]
    d_press = mm(ld, split3(part[0]))
    mixed = []
    for r in range(3):
        w = jac[3 * r:3 * r + 1] * part[1]
        for d in range(1, 3):
            w = w + jac[3 * r + d:3 * r + d + 1] * part[1 + d]
        mixed.append(split3(w))
    diverg = mm(dj, jnp.concatenate(mixed, axis=0))[:BR]
    rates = [diverg - damp * part[0]]
    for d in range(3):
        g = jac[9 + d:10 + d] * d_press[:BR]
        for r in range(1, 3):
            g = g + jac[9 + 3 * r + d:10 + 3 * r + d] * d_press[r * BR:(r + 1) * BR]
        rates.append(g - damp * part[1 + d])
    return jnp.concatenate(rates, axis=1)


def combine(terms, start_time, end_time):
    total = None
    for w, t in zip(weights(start_time, end_time), terms):
        total = w * t if total is None else total + w * t
    return total


def traces(x, pf, width):
    t = mm(pf, split3(x))
    cols = []
    for f in range(4):
        rows = [t[f * KR:(f + 1) * KR, q * width:(q + 1) * width] for q in range(NQ)]
        cols.append(jnp.concatenate(rows, axis=0))
    return cols


def gather(x, onehot):
    hi, lo = hi_lo(x)
    out = mm(jnp.concatenate([hi, lo], axis=0).astype(bf16), onehot)
    n = x.shape[0]
    return out[:n] + out[n:]


def lift(jumps, coef, lf, width, stride):
    flux = [[] for _ in range(NQ)]
    for f in range(4):
        c = coef[:, f * stride:f * stride + width]
        jp = jumps[f][:KR]
        ju = [jumps[f][(1 + d) * KR:(2 + d) * KR] for d in range(3)]
        lam = c[6:7]
        g = c[0:1] * ju[0]
        for d in range(1, 3):
            g = g + c[d:d + 1] * ju[d]
        flux[0].append(g - lam * jp)
        for d in range(3):
            flux[1 + d].append(c[3 + d:4 + d] * jp - lam * ju[d])
    cat = jnp.concatenate([jnp.concatenate(fl, axis=0) for fl in flux], axis=1)
    return mm(lf, split3(cat))[:BR]


def block_mask(shape, block):
    return lax.broadcasted_iota(jnp.int32, shape, 1) // 32 == block


def turn(x, blocks):
    blocks %= 4
    return pltpu.roll(x, 32 * blocks, 1) if blocks else x


def write_parts(refs, sent):
    m_a, m_w, m_1, m_2, m_3, m_own = refs
    m_a[...] = sent[:, :LANES]
    m_w[...] = sent[:, LANES:2 * LANES]
    sub = sent[:, 2 * LANES:]
    for k, ref in ((1, m_1), (2, m_2), (3, m_3)):
        msg = turn(sub[:KR], -k)
        for q in range(1, NQ):
            msg = jnp.where(block_mask(msg.shape, q), turn(sub[q * KR:(q + 1) * KR], q - k), msg)
        ref[...] = msg
    m_own[...] = sub


def received(refs, inner):
    a, w, s1, s2, s3 = [refs[TAKEN.index(i)][...] for i in range(5)]
    own = refs[5][...]
    w = jnp.where(inner[0:1] > 0.5, w, jnp.zeros_like(w))
    rows = []
    for q in range(NQ):
        row = own[q * KR:(q + 1) * KR]
        for k, msg in ((1, s1), (2, s2), (3, s3)):
            row = jnp.where(block_mask(row.shape, k), turn(msg, k - q), row)
        rows.append(row)
    return jnp.concatenate([a, w, jnp.concatenate(rows, axis=0)], axis=1)


def first_kernel(n_elem, n_dom, *refs):
    raw = refs[:13]
    (o_ld, o_dj, o_pf, o_lf, o_coef, o_jac, o_soh, o_at, o_in, o_x, o_xh, o_ph, o_c1, o_c2, o_cs,
     o_t0, m_a, m_w, m_1, m_2, m_3, m_own) = refs[13:35]
    held, sem, pad, lists = refs[35:48], refs[48], refs[49], refs[50]
    copies = [
        pltpu.make_async_copy(src, dst, sem.at[i]) for i, (src, dst) in enumerate(zip(raw, held))
    ]
    for c in copies:
        c.start()
    (start, inv_jac, normals, bulk, density, deriv, proj, liftm, cluster, pml, neighbours,
     dom_send, sub_send) = held
    pad[...] = jnp.zeros_like(pad)
    o_x[...] = jnp.zeros_like(o_x)
    for c in copies:
        c.wait()
    dom_id, sub_id = lax.axis_index("dom"), lax.axis_index("sub")
    inner = jnp.logical_and(dom_id > 0, dom_id < n_dom - 1)
    o_in[...] = jnp.full(o_in.shape, jnp.where(inner, 1.0, 0.0).astype(f32), f32)
    for r in range(3):
        pad[r * BR:r * BR + NB, :NB] = deriv[r]
    hi, lo = hi_lo(pad[:3 * BR])
    left = hi + pltpu.roll(hi, BR, 1) + pltpu.roll(lo, 2 * BR, 1)
    zero8 = jnp.zeros((8, LANES), f32)
    ld = jnp.concatenate([left, zero8], axis=0).astype(bf16)
    dj = jnp.concatenate(
        [jnp.concatenate([left[r * BR:(r + 1) * BR], zero8], axis=0) for r in range(3)], axis=1
    ).astype(bf16)
    pad[...] = jnp.zeros_like(pad)
    for f in range(4):
        pad[f * KR:f * KR + NF, :NB] = proj[:, f, :]
    hi, lo = hi_lo(pad[:4 * KR])
    pf = (hi + pltpu.roll(hi, BR, 1) + pltpu.roll(lo, 2 * BR, 1)).astype(bf16)
    pad[...] = jnp.zeros_like(pad)
    for f in range(4):
        pad[f * KR:f * KR + NF, :NB] = liftm[:, f, :]
    full = jnp.transpose(pad[:LANES])[:48]
    hi, lo = hi_lo(full)
    lf = jnp.concatenate([hi + pltpu.roll(hi, 64, 1), lo], axis=1).astype(bf16)
    o_ld[...] = ld
    o_dj[...] = dj
    o_pf[...] = pf
    o_lf[...] = lf
    bulk_row = bulk[...].reshape(1, n_elem)
    dens_row = density[...].reshape(1, n_elem)
    fine = jnp.where(cluster[...].reshape(1, n_elem) == 1, 1.0, 0.0).astype(f32)
    damp = sigma_pml * pml[...].reshape(1, n_elem).astype(f32)
    jac_in = inv_jac[...]
    o_jac[0:9] = -bulk_row * jac_in
    o_jac[9:18] = -jac_in / dens_row
    o_jac[18:19] = damp
    o_jac[19:20] = fine
    o_jac[20:24] = jnp.zeros((4, n_elem), f32)
    speed = jnp.sqrt(bulk_row / dens_row)
    for f in range(4):
        n = normals[3 * f:3 * f + 3]
        lanes = pl.ds(f * n_elem, n_elem)
        o_coef[0:3, lanes] = 0.5 * bulk_row * n
        o_coef[3:6, lanes] = 0.5 * n / dens_row
        o_coef[6:7, lanes] = 0.5 * speed * jnp.sqrt(jnp.sum(n * n, axis=0, keepdims=True))
        o_coef[7:8, lanes] = jnp.zeros((1, n_elem), f32)
    for q in range(NQ):
        o_x[:NB, q * n_elem:(q + 1) * n_elem] = start[q * NB:(q + 1) * NB]
    x = o_x[...]
    jac = o_jac[...]
    terms = [x]
    for _ in range(ORDER - 1):
        terms.append(apply_l(terms[-1], jac, ld, dj, n_elem))
    p0 = combine(terms, 0.0, SUB_DT)
    o_xh[...] = head(x, n_elem)
    o_ph[...] = head(p0, n_elem)
    o_c1[...] = combine(terms, SUB_DT, 2 * SUB_DT)
    o_c2[...] = combine(terms, 2 * SUB_DT, 3 * SUB_DT)
    o_cs[...] = combine(terms, 0.0, step_size)
    t0 = jnp.concatenate(traces(p0, pf, n_elem), axis=1)
    o_t0[...] = t0
    lists[...] = jnp.full(lists.shape, -1, jnp.int32)
    even = dom_id % 2 == 0
    before, after = dom_send[0:1], dom_send[1:2]
    n_halo = before.shape[1]
    lists[0:1, :n_halo] = jnp.where(even, after, before)
    lists[0:1, LANES:LANES + n_halo] = jnp.where(even, before, after)
    for b in range(4):
        lists[0:1, 2 * LANES + 32 * b:2 * LANES + 32 * (b + 1)] = sub_send[pl.ds(sub_id ^ b, 1)]
    names = lists[0:1]
    n_face = 4 * n_elem
    step = 256
    for j in range(0, n_face, step):
        row = j + lax.broadcasted_iota(jnp.int32, (step, 3 * LANES), 0)
        o_soh[j:j + step] = jnp.where(row == names, 1.0, 0.0).astype(bf16)
    write_parts((m_a, m_w, m_1, m_2, m_3, m_own), gather(t0, o_soh[...]))
    nbr = neighbours[...]
    before_at = jnp.where(even, n_face + LANES, n_face)
    after_at = jnp.where(even, n_face, n_face + LANES)
    slot = nbr - (n_face + 2 * n_halo)
    o_at[...] = jnp.where(
        nbr < n_face,
        nbr,
        jnp.where(
            nbr < n_face + n_halo,
            nbr - n_face + before_at,
            jnp.where(
                nbr < n_face + 2 * n_halo,
                nbr - (n_face + n_halo) + after_at,
                n_face + 2 * LANES + 32 * ((slot >> 5) ^ sub_id) + (slot & 31),
            ),
        ),
    )


def fine_base(state, pub, t, roh, coef, jac, ld, dj, lf, n_elem):
    tile = LANES
    jumps = []
    for f in range(4):
        own = t[:, f * n_elem:f * n_elem + tile]
        got = gather(t, roh[:4 * n_elem, f * tile:(f + 1) * tile])
        jumps.append(got - own)
    corr = lift(jumps, coef, lf, tile, n_elem)
    return state + apply_l(pub, jac, ld, dj, tile) - corr


def head(x, n_elem):
    return jnp.concatenate(
        [x[:, q * n_elem:q * n_elem + LANES] for q in range(NQ)], axis=1
    )


def table(at, roh, n_elem, first, count):
    step = 128
    for f in range(4):
        col = at[f:f + 1, first:first + count]
        for j in range(0, roh.shape[0], step):
            row = j + lax.broadcasted_iota(jnp.int32, (step, count), 0)
            roh[j:j + step, f * count:(f + 1) * count] = jnp.where(row == col, 1.0, 0.0).astype(bf16)


def coarse_traces(c, soh, jac, pf, o_t, o_s, n_elem):
    fine4 = jnp.concatenate([jac[19:20]] * 4, axis=1)
    t = jnp.concatenate(traces(c[...], pf[...], n_elem), axis=1)
    t = jnp.where(fine4 > 0.5, 0.0, t)
    o_t[...] = t
    o_s[...] = gather(t, soh[...])


def window0_kernel(n_elem, at, xh, ph, c1, t0, soh, coef, jac, ld, dj, pf, lf,
                   roh, o_base, o_t1, o_s1):
    table(at, roh, n_elem, 0, LANES)
    o_base[...] = fine_base(xh[...], ph[...], t0[...], roh, coef[...], jac[:, :LANES], ld[...],
                            dj[...], lf[...], n_elem)
    coarse_traces(c1, soh, jac, pf, o_t1, o_s1, n_elem)


def step_kernel(n_elem, last,
                inner, r_a, r_w, r_1, r_2, r_3, r_own, base, p_sum, t_coarse, s_coarse,
                roh, soh, coef, jac, ld, dj, pf, lf,
                *outs):
    o_sum, o_t, m_a, m_w, m_1, m_2, m_3, m_own = outs[:8]
    n_face = 4 * n_elem
    tile = LANES
    got = received((r_a, r_w, r_1, r_2, r_3, r_own), inner[...])
    jumps = [gather(got, roh[n_face:, f * tile:(f + 1) * tile]) for f in range(4)]
    state = base[...] - lift(jumps, coef[...], lf[...], tile, n_elem)
    jac_h = jac[:, :tile]
    terms = [state]
    for _ in range(ORDER - 1):
        terms.append(apply_l(terms[-1], jac_h, ld[...], dj[...], tile))
    pub = combine(terms, 0.0, SUB_DT)
    total = p_sum[...] + pub
    o_sum[...] = total
    if not last:
        outs[8][...] = state
        outs[9][...] = pub
    fine = jac_h[19:20] > 0.5
    zero = jnp.zeros((4 * KR, tile), f32)
    fine_t = [jnp.where(fine, t, zero) for t in traces(total if last else pub, pf[...], tile)]
    o_t[...] = t_coarse[...]
    for f in range(4):
        o_t[:, f * n_elem:f * n_elem + tile] += fine_t[f]
    sent = s_coarse[...]
    for f in range(4):
        sent = sent + gather(fine_t[f], soh[f * n_elem:f * n_elem + tile])
    write_parts((m_a, m_w, m_1, m_2, m_3, m_own), sent)


def window_kernel(n_elem, tabled, at, state, pub, t, c, roh, soh, coef, jac, ld, dj, pf, lf,
                  o_base, o_t, o_s, *o_roh):
    o_base[...] = fine_base(state[...], pub[...], t[...], roh, coef[...], jac[:, :LANES], ld[...],
                            dj[...], lf[...], n_elem)
    coarse_traces(c, soh, jac, pf, o_t, o_s, n_elem)
    if tabled:
        table(at, o_roh[0], n_elem, LANES, n_elem - LANES)


def split_gather(x, roh, roh2, rows, f, n_elem):
    rest = n_elem - LANES
    return jnp.concatenate(
        [gather(x, roh[rows, f * LANES:(f + 1) * LANES]), gather(x, roh2[rows, f * rest:(f + 1) * rest])],
        axis=1,
    )


def window3_kernel(n_elem, x, cs, total, t, roh, roh2, coef, jac, ld, dj, lf, o_base):
    fine = jac[19:20, :LANES] > 0.5
    parts = []
    for q in range(NQ):
        c = cs[:, q * n_elem:(q + 1) * n_elem]
        parts.append(jnp.where(fine, total[:, q * LANES:(q + 1) * LANES], c[:, :LANES]))
        parts.append(c[:, LANES:])
    pub = jnp.concatenate(parts, axis=1)
    tv = t[...]
    rows = slice(0, 4 * n_elem)
    jumps = [
        split_gather(tv, roh, roh2, rows, f, n_elem) - tv[:, f * n_elem:(f + 1) * n_elem]
        for f in range(4)
    ]
    corr = lift(jumps, coef[...], lf[...], n_elem, n_elem)
    o_base[...] = x[...] + apply_l(pub, jac[...], ld[...], dj[...], n_elem) - corr


def last_kernel(n_elem, inner, r_a, r_w, r_1, r_2, r_3, r_own, base, roh, roh2, coef, lf, out):
    got = received((r_a, r_w, r_1, r_2, r_3, r_own), inner[...])
    rows = slice(4 * n_elem, 4 * n_elem + 3 * LANES)
    jumps = [split_gather(got, roh, roh2, rows, f, n_elem) for f in range(4)]
    res = base[...] - lift(jumps, coef[...], lf[...], n_elem, n_elem)
    for q in range(NQ):
        out[q * NB:(q + 1) * NB] = res[:NB, q * n_elem:(q + 1) * n_elem]


def call(kernel, name, outs, args, scratch=(), raw=(), hbm_out=False, flops=0):
    vm = pl.BlockSpec(memory_space=pltpu.VMEM)
    specs, ops = [], []
    for i, a in enumerate(args):
        if i in raw:
            specs.append(pl.BlockSpec(memory_space=pltpu.HBM))
            ops.append(pltpu.with_memory_space_constraint(a, pltpu.HBM))
        else:
            specs.append(vm)
            ops.append(pltpu.with_memory_space_constraint(a, pltpu.VMEM))
    shapes = [
        jax.ShapeDtypeStruct(s, d) if hbm_out else pltpu.VMEM(s, d) for s, d in outs
    ]
    return pl.pallas_call(
        kernel,
        in_specs=specs,
        out_specs=[vm] * len(shapes),
        out_shape=shapes,
        scratch_shapes=list(scratch),
        name=name,
        compiler_params=pltpu.CompilerParams(vmem_limit_bytes=16 << 20),
        cost_estimate=pl.CostEstimate(flops=flops, bytes_accessed=1 << 16, transcendentals=0),
    )(*ops)


TAKEN = (4, 3, 2, 1, 0)


def exchange(parts, n_dom):
    a, w, s1, s2, s3, own = parts
    other = [(i, ((i + 1) ^ 1) - 1 if 0 < i < n_dom - 1 else n_dom - 1 - i) for i in range(n_dom)]
    r1 = lax.ppermute(s1, "sub", [(i, i ^ 1) for i in range(4)])
    ra = lax.ppermute(a, "dom", [(i, i ^ 1) for i in range(n_dom)])
    r3 = lax.ppermute(s3, "sub", [(i, i ^ 3) for i in range(4)])
    rw = lax.ppermute(w, "dom", other)
    r2 = lax.ppermute(s2, "sub", [(i, i ^ 2) for i in range(4)])
    got = (ra, rw, r1, r2, r3)
    return tuple(got[i] for i in TAKEN) + (own,)


def make_body(n_dom, n_sub):
    assert n_dom % 2 == 0 and n_sub == 4

    def body(start_dofs, inv_jac, normals, bulk_modulus, density, deriv_mats, face_proj, face_lift,
             cluster, pml_flags, neighbours, dom_send, sub_send):
        n_elem = start_dofs.shape[1]
        n_halo = dom_send.shape[1]
        n_face = 4 * n_elem
        wide = ((BR, NQ * n_elem), f32)
        slim = ((BR, NQ * LANES), f32)
        trace = ((4 * KR, n_face), f32)
        listed = ((4 * KR, 3 * LANES), f32)
        msg = ((4 * KR, LANES), f32)
        small = ((KR, LANES), f32)
        msg_row = ((8, LANES), f32)
        msgs = [msg, msg, small, small, small, msg]
        half = ((n_face + 3 * LANES, 4 * LANES), bf16)
        rest = ((n_face + 3 * LANES, 4 * (n_elem - LANES)), bf16)
        raw = [start_dofs, inv_jac, normals, bulk_modulus, density, deriv_mats,
               jnp.transpose(face_proj, (1, 0, 2)), jnp.transpose(face_lift, (2, 0, 1)),
               cluster, pml_flags, neighbours, dom_send, sub_send]
        first = call(
            lambda *r: first_kernel(n_elem, n_dom, *r), "first",
            [((128, 128), bf16), ((48, 384), bf16), ((64, 128), bf16), ((48, 256), bf16),
             ((8, n_face), f32), ((24, n_elem), f32), ((n_face, 3 * LANES), bf16),
             ((4, n_elem), jnp.int32), msg_row, wide, slim, slim, wide, wide, wide, trace] + msgs,
            raw, raw=range(13),
            scratch=[pltpu.VMEM(a.shape, a.dtype) for a in raw]
            + [pltpu.SemaphoreType.DMA((len(raw),)), pltpu.VMEM((128, LANES), f32),
               pltpu.VMEM((8, 3 * LANES), jnp.int32)],
        )
        ld, dj, pf, lf, coef, jac, soh, at, inner, x, xh, total, c1, c2, cs, t = first[:16]
        got = exchange(first[16:], n_dom)
        roh, base, t_c, s_c = call(
            lambda *r: window0_kernel(n_elem, *r), "window0", [half, slim, trace, listed],
            [at, xh, total, c1, t, soh, coef, jac, ld, dj, pf, lf], flops=1 << 28,
        )
        roh2 = None
        for s in range(SUBSTEPS - 1):
            last = s == SUBSTEPS - 2
            outs = call(
                lambda *r, last=last: step_kernel(n_elem, last, *r), "step",
                [slim, trace] + msgs + ([] if last else [slim] * 2),
                [inner, *got, base, total, t_c, s_c, roh, soh, coef, jac, ld, dj, pf, lf],
            )
            total, t = outs[:2]
            got = exchange(outs[2:8], n_dom)
            if last:
                (base,) = call(
                    lambda *r: window3_kernel(n_elem, *r), "window3", [wide],
                    [x, cs, total, t, roh, roh2, coef, jac, ld, dj, lf], flops=1 << 28,
                )
            else:
                res = call(
                    lambda *r, s=s: window_kernel(n_elem, s == 0, *r), "window",
                    [slim, trace, listed] + ([rest] if s == 0 else []),
                    [at, outs[8], outs[9], t, (c2, cs)[s], roh, soh, coef, jac, ld, dj, pf, lf],
                    flops=1 << 28,
                )
                base, t_c, s_c = res[:3]
                if s == 0:
                    roh2 = res[3]
        (out,) = call(
            lambda *r: last_kernel(n_elem, *r), "last",
            [((NQ * NB, n_elem), f32)], [inner, *got, base, roh, roh2, coef, lf], hbm_out=True,
        )
        return out

    return body


def solution(mesh):
    in_specs = (
        P(None, ("dom", "sub")),
        P(None, ("dom", "sub")),
        P(None, ("dom", "sub")),
        P(("dom", "sub")),
        P(("dom", "sub")),
        P(),
        P(),
        P(),
        P(("dom", "sub")),
        P(("dom", "sub")),
        P(None, ("dom", "sub")),
        P(("dom", "sub"), None),
        P(("dom", "sub"), None),
    )
    out_specs = P(None, ("dom", "sub"))
    body = make_body(mesh.shape["dom"], mesh.shape["sub"])
    return jax.shard_map(body, mesh=mesh, in_specs=in_specs, out_specs=out_specs, check_vma=False)
```

```python
import math

import jax
import jax.numpy as jnp
from jax import lax
from jax.experimental import pallas as pl
from jax.experimental.pallas import tpu as pltpu
from jax.sharding import PartitionSpec as P

NQ = 4
NB = 35
NF = 15
ORDER = 5
SUBSTEPS = 4
BR = 40
KR = 16
LANES = 128

step_size = 0.8
sigma_pml = 1.5
f32 = jnp.float32
bf16 = jnp.bfloat16


def weights(start_time, end_time):
    return [
        (end_time ** (k + 1) - start_time ** (k + 1)) / math.factorial(k + 1)
        for k in range(ORDER)
    ]


SUB_DT = step_size / SUBSTEPS


def hi_lo(x):
    hi = x.astype(bf16).astype(f32)
    return hi, x - hi


def split3(x):
    hi, lo = hi_lo(x)
    parts = [hi, lo, hi]
    pad = -3 * x.shape[0] % LANES
    if pad:
        parts.append(jnp.zeros((pad, x.shape[1]), f32))
    return jnp.concatenate(parts, axis=0).astype(bf16)


def mm(a, b):
    return jnp.dot(a, b, preferred_element_type=f32)


def apply_l(x, jac, ld, dj, width):
    part = [x[:, q * width:(q + 1) * width] for q in range(NQ)]
    damp = jac[18:19]
    d_press = mm(ld, split3(part[0]))
    mixed = []
    for r in range(3):
        w = jac[3 * r:3 * r + 1] * part[1]
        for d in range(1, 3):
            w = w + jac[3 * r + d:3 * r + d + 1] * part[1 + d]
        mixed.append(split3(w))
    diverg = mm(dj, jnp.concatenate(mixed, axis=0))[:BR]
    rates = [diverg - damp * part[0]]
    for d in range(3):
        g = jac[9 + d:10 + d] * d_press[:BR]
        for r in range(1, 3):
            g = g + jac[9 + 3 * r + d:10 + 3 * r + d] * d_press[r * BR:(r + 1) * BR]
        rates.append(g - damp * part[1 + d])
    return jnp.concatenate(rates, axis=1)


def combine(terms, start_time, end_time):
    total = None
    for w, t in zip(weights(start_time, end_time), terms):
        total = w * t if total is None else total + w * t
    return total


def traces(x, pf, width):
    t = mm(pf, split3(x))
    cols = []
    for f in range(4):
        rows = [t[f * KR:(f + 1) * KR, q * width:(q + 1) * width] for q in range(NQ)]
        cols.append(jnp.concatenate(rows, axis=0))
    return cols


def gather(x, onehot):
    hi, lo = hi_lo(x)
    out = mm(jnp.concatenate([hi, lo], axis=0).astype(bf16), onehot)
    n = x.shape[0]
    return out[:n] + out[n:]


def lift(jumps, coef, lf, width, stride):
    flux = [[] for _ in range(NQ)]
    for f in range(4):
        c = coef[:, f * stride:f * stride + width]
        jp = jumps[f][:KR]
        ju = [jumps[f][(1 + d) * KR:(2 + d) * KR] for d in range(3)]
        lam = c[6:7]
        g = c[0:1] * ju[0]
        for d in range(1, 3):
            g = g + c[d:d + 1] * ju[d]
        flux[0].append(g - lam * jp)
        for d in range(3):
            flux[1 + d].append(c[3 + d:4 + d] * jp - lam * ju[d])
    cat = jnp.concatenate([jnp.concatenate(fl, axis=0) for fl in flux], axis=1)
    return mm(lf, split3(cat))[:BR]


def block_mask(shape, block):
    return lax.broadcasted_iota(jnp.int32, shape, 1) // 32 == block


def turn(x, blocks):
    blocks %= 4
    return pltpu.roll(x, 32 * blocks, 1) if blocks else x


def write_parts(refs, sent):
    m_a, m_w, m_1, m_2, m_3, m_own = refs
    for i, ref in ((0, m_a), (1, m_w)):
        part = sent[:, i * LANES:(i + 1) * LANES]
        for q in range(3):
            row = part[q * KR:(q + 1) * KR]
            ref[q * KR:(q + 1) * KR] = jnp.where(block_mask(row.shape, 3), turn(part[3 * KR:], 3 - q), row)
    sub = sent[:, 2 * LANES:]
    for k, ref in ((1, m_1), (2, m_2), (3, m_3)):
        msg = turn(sub[:KR], -k)
        for q in range(1, NQ):
            msg = jnp.where(block_mask(msg.shape, q), turn(sub[q * KR:(q + 1) * KR], q - k), msg)
        ref[:KR] = msg
    m_own[...] = sub


def unpack(msg):
    last = turn(msg[2 * KR:], -1)
    for q in (1, 0):
        last = jnp.where(block_mask(last.shape, q), turn(msg[q * KR:(q + 1) * KR], q - 3), last)
    return jnp.concatenate([msg, last], axis=0)


def received(refs, inner):
    a, w, s1, s2, s3 = [refs[TAKEN.index(i)] for i in range(5)]
    own = refs[5][...]
    a = unpack(a[...])
    w = unpack(w[...])
    w = jnp.where(inner[0:1] > 0.5, w, jnp.zeros_like(w))
    s1, s2, s3 = s1[:KR], s2[:KR], s3[:KR]
    rows = []
    for q in range(NQ):
        row = own[q * KR:(q + 1) * KR]
        for k, msg in ((1, s1), (2, s2), (3, s3)):
            row = jnp.where(block_mask(row.shape, k), turn(msg, k - q), row)
        rows.append(row)
    return jnp.concatenate([a, w, jnp.concatenate(rows, axis=0)], axis=1)


def first_kernel(n_elem, n_dom, *refs):
    raw = refs[:13]
    (o_ld, o_dj, o_pf, o_lf, o_coef, o_jac, o_soh, o_at, o_in, o_x, o_xh, o_ph, o_c1, o_c2, o_cs,
     o_t0, m_a, m_w, m_1, m_2, m_3, m_own) = refs[13:35]
    held, sem, pad, lists = refs[35:48], refs[48], refs[49], refs[50]
    copies = [
        pltpu.make_async_copy(src, dst, sem.at[i]) for i, (src, dst) in enumerate(zip(raw, held))
    ]
    for c in copies:
        c.start()
    (start, inv_jac, normals, bulk, density, deriv, proj, liftm, cluster, pml, neighbours,
     dom_send, sub_send) = held
    pad[...] = jnp.zeros_like(pad)
    o_x[...] = jnp.zeros_like(o_x)
    for c in copies:
        c.wait()
    dom_id, sub_id = lax.axis_index("dom"), lax.axis_index("sub")
    inner = jnp.logical_and(dom_id > 0, dom_id < n_dom - 1)
    o_in[...] = jnp.full(o_in.shape, jnp.where(inner, 1.0, 0.0).astype(f32), f32)
    for r in range(3):
        pad[r * BR:r * BR + NB, :NB] = deriv[r]
    hi, lo = hi_lo(pad[:3 * BR])
    left = hi + pltpu.roll(hi, BR, 1) + pltpu.roll(lo, 2 * BR, 1)
    zero8 = jnp.zeros((8, LANES), f32)
    ld = jnp.concatenate([left, zero8], axis=0).astype(bf16)
    dj = jnp.concatenate(
        [jnp.concatenate([left[r * BR:(r + 1) * BR], zero8], axis=0) for r in range(3)], axis=1
    ).astype(bf16)
    pad[...] = jnp.zeros_like(pad)
    for f in range(4):
        pad[f * KR:f * KR + NF, :NB] = proj[:, f, :]
    hi, lo = hi_lo(pad[:4 * KR])
    pf = (hi + pltpu.roll(hi, BR, 1) + pltpu.roll(lo, 2 * BR, 1)).astype(bf16)
    pad[...] = jnp.zeros_like(pad)
    for f in range(4):
        pad[f * KR:f * KR + NF, :NB] = liftm[:, f, :]
    full = jnp.transpose(pad[:LANES])[:48]
    hi, lo = hi_lo(full)
    lf = jnp.concatenate([hi + pltpu.roll(hi, 64, 1), lo], axis=1).astype(bf16)
    o_ld[...] = ld
    o_dj[...] = dj
    o_pf[...] = pf
    o_lf[...] = lf
    bulk_row = bulk[...].reshape(1, n_elem)
    dens_row = density[...].reshape(1, n_elem)
    fine = jnp.where(cluster[...].reshape(1, n_elem) == 1, 1.0, 0.0).astype(f32)
    damp = sigma_pml * pml[...].reshape(1, n_elem).astype(f32)
    jac_in = inv_jac[...]
    o_jac[0:9] = -bulk_row * jac_in
    o_jac[9:18] = -jac_in / dens_row
    o_jac[18:19] = damp
    o_jac[19:20] = fine
    o_jac[20:24] = jnp.zeros((4, n_elem), f32)
    speed = jnp.sqrt(bulk_row / dens_row)
    for f in range(4):
        n = normals[3 * f:3 * f + 3]
        lanes = pl.ds(f * n_elem, n_elem)
        o_coef[0:3, lanes] = 0.5 * bulk_row * n
        o_coef[3:6, lanes] = 0.5 * n / dens_row
        o_coef[6:7, lanes] = 0.5 * speed * jnp.sqrt(jnp.sum(n * n, axis=0, keepdims=True))
        o_coef[7:8, lanes] = jnp.zeros((1, n_elem), f32)
    for q in range(NQ):
        o_x[:NB, q * n_elem:(q + 1) * n_elem] = start[q * NB:(q + 1) * NB]
    x = o_x[...]
    jac = o_jac[...]
    terms = [x]
    for _ in range(ORDER - 1):
        terms.append(apply_l(terms[-1], jac, ld, dj, n_elem))
    p0 = combine(terms, 0.0, SUB_DT)
    o_xh[...] = head(x, n_elem)
    o_ph[...] = head(p0, n_elem)
    o_c1[...] = combine(terms, SUB_DT, 2 * SUB_DT)
    o_c2[...] = combine(terms, 2 * SUB_DT, 3 * SUB_DT)
    o_cs[...] = combine(terms, 0.0, step_size)
    t0 = jnp.concatenate(traces(p0, pf, n_elem), axis=1)
    o_t0[...] = t0
    lists[...] = jnp.full(lists.shape, -1, jnp.int32)
    even = dom_id % 2 == 0
    before, after = dom_send[0:1], dom_send[1:2]
    n_halo = before.shape[1]
    lists[0:1, :n_halo] = jnp.where(even, after, before)
    lists[0:1, LANES:LANES + n_halo] = jnp.where(even, before, after)
    for b in range(4):
        lists[0:1, 2 * LANES + 32 * b:2 * LANES + 32 * (b + 1)] = sub_send[pl.ds(sub_id ^ b, 1)]
    names = lists[0:1]
    n_face = 4 * n_elem
    step = 256
    for j in range(0, n_face, step):
        row = j + lax.broadcasted_iota(jnp.int32, (step, 3 * LANES), 0)
        o_soh[j:j + step] = jnp.where(row == names, 1.0, 0.0).astype(bf16)
    write_parts((m_a, m_w, m_1, m_2, m_3, m_own), gather(t0, o_soh[...]))
    nbr = neighbours[...]
    before_at = jnp.where(even, n_face + LANES, n_face)
    after_at = jnp.where(even, n_face, n_face + LANES)
    slot = nbr - (n_face + 2 * n_halo)
    o_at[...] = jnp.where(
        nbr < n_face,
        nbr,
        jnp.where(
            nbr < n_face + n_halo,
            nbr - n_face + before_at,
            jnp.where(
                nbr < n_face + 2 * n_halo,
                nbr - (n_face + n_halo) + after_at,
                n_face + 2 * LANES + 32 * ((slot >> 5) ^ sub_id) + (slot & 31),
            ),
        ),
    )


def fine_base(state, pub, t, roh, coef, jac, ld, dj, lf, n_elem):
    tile = LANES
    jumps = []
    for f in range(4):
        own = t[:, f * n_elem:f * n_elem + tile]
        got = gather(t, roh[:4 * n_elem, f * tile:(f + 1) * tile])
        jumps.append(got - own)
    corr = lift(jumps, coef, lf, tile, n_elem)
    return state + apply_l(pub, jac, ld, dj, tile) - corr


def head(x, n_elem):
    return jnp.concatenate(
        [x[:, q * n_elem:q * n_elem + LANES] for q in range(NQ)], axis=1
    )


def table(at, roh, n_elem, first, count):
    step = 128
    for f in range(4):
        col = at[f:f + 1, first:first + count]
        for j in range(0, roh.shape[0], step):
            row = j + lax.broadcasted_iota(jnp.int32, (step, count), 0)
            roh[j:j + step, f * count:(f + 1) * count] = jnp.where(row == col, 1.0, 0.0).astype(bf16)


def coarse_traces(c, soh, jac, pf, o_t, o_s, n_elem):
    fine4 = jnp.concatenate([jac[19:20]] * 4, axis=1)
    t = jnp.concatenate(traces(c[...], pf[...], n_elem), axis=1)
    t = jnp.where(fine4 > 0.5, 0.0, t)
    o_t[...] = t
    o_s[...] = gather(t, soh[...])


def window0_kernel(n_elem, at, xh, ph, c1, t0, soh, coef, jac, ld, dj, pf, lf,
                   roh, o_base, o_t1, o_s1):
    table(at, roh, n_elem, 0, LANES)
    o_base[...] = fine_base(xh[...], ph[...], t0[...], roh, coef[...], jac[:, :LANES], ld[...],
                            dj[...], lf[...], n_elem)
    coarse_traces(c1, soh, jac, pf, o_t1, o_s1, n_elem)


def step_kernel(n_elem, last,
                inner, r_a, r_w, r_1, r_2, r_3, r_own, base, p_sum, t_coarse, s_coarse,
                roh, soh, coef, jac, ld, dj, pf, lf,
                *outs):
    o_sum, o_t, m_a, m_w, m_1, m_2, m_3, m_own = outs[:8]
    n_face = 4 * n_elem
    tile = LANES
    got = received((r_a, r_w, r_1, r_2, r_3, r_own), inner[...])
    jumps = [gather(got, roh[n_face:, f * tile:(f + 1) * tile]) for f in range(4)]
    state = base[...] - lift(jumps, coef[...], lf[...], tile, n_elem)
    jac_h = jac[:, :tile]
    terms = [state]
    for _ in range(ORDER - 1):
        terms.append(apply_l(terms[-1], jac_h, ld[...], dj[...], tile))
    pub = combine(terms, 0.0, SUB_DT)
    total = p_sum[...] + pub
    o_sum[...] = total
    if not last:
        outs[8][...] = state
        outs[9][...] = pub
    fine = jac_h[19:20] > 0.5
    zero = jnp.zeros((4 * KR, tile), f32)
    fine_t = [jnp.where(fine, t, zero) for t in traces(total if last else pub, pf[...], tile)]
    o_t[...] = t_coarse[...]
    for f in range(4):
        o_t[:, f * n_elem:f * n_elem + tile] += fine_t[f]
    sent = s_coarse[...]
    for f in range(4):
        sent = sent + gather(fine_t[f], soh[f * n_elem:f * n_elem + tile])
    write_parts((m_a, m_w, m_1, m_2, m_3, m_own), sent)


def window_kernel(n_elem, tabled, at, state, pub, t, c, roh, soh, coef, jac, ld, dj, pf, lf,
                  o_base, o_t, o_s, *o_roh):
    o_base[...] = fine_base(state[...], pub[...], t[...], roh, coef[...], jac[:, :LANES], ld[...],
                            dj[...], lf[...], n_elem)
    coarse_traces(c, soh, jac, pf, o_t, o_s, n_elem)
    if tabled:
        table(at, o_roh[0], n_elem, LANES, n_elem - LANES)


def split_gather(x, roh, roh2, rows, f, n_elem):
    rest = n_elem - LANES
    return jnp.concatenate(
        [gather(x, roh[rows, f * LANES:(f + 1) * LANES]), gather(x, roh2[rows, f * rest:(f + 1) * rest])],
        axis=1,
    )


def window3_kernel(n_elem, x, cs, total, t, roh, roh2, coef, jac, ld, dj, lf, o_base):
    fine = jac[19:20, :LANES] > 0.5
    parts = []
    for q in range(NQ):
        c = cs[:, q * n_elem:(q + 1) * n_elem]
        parts.append(jnp.where(fine, total[:, q * LANES:(q + 1) * LANES], c[:, :LANES]))
        parts.append(c[:, LANES:])
    pub = jnp.concatenate(parts, axis=1)
    tv = t[...]
    rows = slice(0, 4 * n_elem)
    jumps = [
        split_gather(tv, roh, roh2, rows, f, n_elem) - tv[:, f * n_elem:(f + 1) * n_elem]
        for f in range(4)
    ]
    corr = lift(jumps, coef[...], lf[...], n_elem, n_elem)
    o_base[...] = x[...] + apply_l(pub, jac[...], ld[...], dj[...], n_elem) - corr


def last_kernel(n_elem, inner, r_a, r_w, r_1, r_2, r_3, r_own, base, roh, roh2, coef, lf, out):
    got = received((r_a, r_w, r_1, r_2, r_3, r_own), inner[...])
    rows = slice(4 * n_elem, 4 * n_elem + 3 * LANES)
    jumps = [split_gather(got, roh, roh2, rows, f, n_elem) for f in range(4)]
    res = base[...] - lift(jumps, coef[...], lf[...], n_elem, n_elem)
    for q in range(NQ):
        out[q * NB:(q + 1) * NB] = res[:NB, q * n_elem:(q + 1) * n_elem]


def call(kernel, name, outs, args, scratch=(), raw=(), hbm_out=False, flops=0):
    vm = pl.BlockSpec(memory_space=pltpu.VMEM)
    specs, ops = [], []
    for i, a in enumerate(args):
        if i in raw:
            specs.append(pl.BlockSpec(memory_space=pltpu.HBM))
            ops.append(pltpu.with_memory_space_constraint(a, pltpu.HBM))
        else:
            specs.append(vm)
            ops.append(pltpu.with_memory_space_constraint(a, pltpu.VMEM))
    shapes = [
        jax.ShapeDtypeStruct(s, d) if hbm_out else pltpu.VMEM(s, d) for s, d in outs
    ]
    return pl.pallas_call(
        kernel,
        in_specs=specs,
        out_specs=[vm] * len(shapes),
        out_shape=shapes,
        scratch_shapes=list(scratch),
        name=name,
        compiler_params=pltpu.CompilerParams(vmem_limit_bytes=16 << 20),
        cost_estimate=pl.CostEstimate(flops=flops, bytes_accessed=1 << 16, transcendentals=0),
    )(*ops)


TAKEN = (4, 3, 1, 2, 0)


def exchange(parts, n_dom):
    a, w, s1, s2, s3, own = parts
    other = [(i, ((i + 1) ^ 1) - 1 if 0 < i < n_dom - 1 else n_dom - 1 - i) for i in range(n_dom)]
    r1 = lax.ppermute(s1, "sub", [(i, i ^ 1) for i in range(4)])
    ra = lax.ppermute(a, "dom", [(i, i ^ 1) for i in range(n_dom)])
    r3 = lax.ppermute(s3, "sub", [(i, i ^ 3) for i in range(4)])
    rw = lax.ppermute(w, "dom", other)
    r2 = lax.ppermute(s2, "sub", [(i, i ^ 2) for i in range(4)])
    got = (ra, rw, r1, r2, r3)
    return tuple(got[i] for i in TAKEN) + (own,)


def make_body(n_dom, n_sub):
    assert n_dom % 2 == 0 and n_sub == 4

    def body(start_dofs, inv_jac, normals, bulk_modulus, density, deriv_mats, face_proj, face_lift,
             cluster, pml_flags, neighbours, dom_send, sub_send):
        n_elem = start_dofs.shape[1]
        n_halo = dom_send.shape[1]
        assert n_halo <= 96
        n_face = 4 * n_elem
        wide = ((BR, NQ * n_elem), f32)
        slim = ((BR, NQ * LANES), f32)
        trace = ((4 * KR, n_face), f32)
        listed = ((4 * KR, 3 * LANES), f32)
        msg = ((4 * KR, LANES), f32)
        small = ((KR, LANES), f32)
        dom_msg = ((3 * KR, LANES), f32)
        msg_row = ((8, LANES), f32)
        msgs = [dom_msg, dom_msg, dom_msg, small, small, msg]
        half = ((n_face + 3 * LANES, 4 * LANES), bf16)
        rest = ((n_face + 3 * LANES, 4 * (n_elem - LANES)), bf16)
        raw = [start_dofs, inv_jac, normals, bulk_modulus, density, deriv_mats,
               jnp.transpose(face_proj, (1, 0, 2)), jnp.transpose(face_lift, (2, 0, 1)),
               cluster, pml_flags, neighbours, dom_send, sub_send]
        first = call(
            lambda *r: first_kernel(n_elem, n_dom, *r), "first",
            [((128, 128), bf16), ((48, 384), bf16), ((64, 128), bf16), ((48, 256), bf16),
             ((8, n_face), f32), ((24, n_elem), f32), ((n_face, 3 * LANES), bf16),
             ((4, n_elem), jnp.int32), msg_row, wide, slim, slim, wide, wide, wide, trace] + msgs,
            raw, raw=range(13),
            scratch=[pltpu.VMEM(a.shape, a.dtype) for a in raw]
            + [pltpu.SemaphoreType.DMA((len(raw),)), pltpu.VMEM((128, LANES), f32),
               pltpu.VMEM((8, 3 * LANES), jnp.int32)],
        )
        ld, dj, pf, lf, coef, jac, soh, at, inner, x, xh, total, c1, c2, cs, t = first[:16]
        got = exchange(first[16:], n_dom)
        roh, base, t_c, s_c = call(
            lambda *r: window0_kernel(n_elem, *r), "window0", [half, slim, trace, listed],
            [at, xh, total, c1, t, soh, coef, jac, ld, dj, pf, lf], flops=1 << 36,
        )
        roh2 = None
        for s in range(SUBSTEPS - 1):
            last = s == SUBSTEPS - 2
            outs = call(
                lambda *r, last=last: step_kernel(n_elem, last, *r), "step",
                [slim, trace] + msgs + ([] if last else [slim] * 2),
                [inner, *got, base, total, t_c, s_c, roh, soh, coef, jac, ld, dj, pf, lf],
            )
            total, t = outs[:2]
            got = exchange(outs[2:8], n_dom)
            if last:
                (base,) = call(
                    lambda *r: window3_kernel(n_elem, *r), "window3", [wide],
                    [x, cs, total, t, roh, roh2, coef, jac, ld, dj, lf], flops=1 << 36,
                )
            else:
                res = call(
                    lambda *r, s=s: window_kernel(n_elem, s == 0, *r), "window",
                    [slim, trace, listed] + ([rest] if s == 0 else []),
                    [at, outs[8], outs[9], t, (c2, cs)[s], roh, soh, coef, jac, ld, dj, pf, lf],
                    flops=1 << 36,
                )
                base, t_c, s_c = res[:3]
                if s == 0:
                    roh2 = res[3]
        (out,) = call(
            lambda *r: last_kernel(n_elem, *r), "last",
            [((NQ * NB, n_elem), f32)], [inner, *got, base, roh, roh2, coef, lf], hbm_out=True,
        )
        return out

    return body


def solution(mesh):
    in_specs = (
        P(None, ("dom", "sub")),
        P(None, ("dom", "sub")),
        P(None, ("dom", "sub")),
        P(("dom", "sub")),
        P(("dom", "sub")),
        P(),
        P(),
        P(),
        P(("dom", "sub")),
        P(("dom", "sub")),
        P(None, ("dom", "sub")),
        P(("dom", "sub"), None),
        P(("dom", "sub"), None),
    )
    out_specs = P(None, ("dom", "sub"))
    body = make_body(mesh.shape["dom"], mesh.shape["sub"])
    return jax.shard_map(body, mesh=mesh, in_specs=in_specs, out_specs=out_specs, check_vma=False)
```

```python
import math

import jax
import jax.numpy as jnp
from jax import lax
from jax.experimental import pallas as pl
from jax.experimental.pallas import tpu as pltpu
from jax.sharding import PartitionSpec as P

NQ = 4
NB = 35
NF = 15
ORDER = 5
SUBSTEPS = 4
BR = 40
KR = 16
LANES = 128

step_size = 0.8
sigma_pml = 1.5
f32 = jnp.float32
bf16 = jnp.bfloat16


def weights(start_time, end_time):
    return [
        (end_time ** (k + 1) - start_time ** (k + 1)) / math.factorial(k + 1)
        for k in range(ORDER)
    ]


SUB_DT = step_size / SUBSTEPS


def hi_lo(x):
    hi = x.astype(bf16).astype(f32)
    return hi, x - hi


def split3(x):
    hi, lo = hi_lo(x)
    parts = [hi, lo, hi]
    pad = -3 * x.shape[0] % LANES
    if pad:
        parts.append(jnp.zeros((pad, x.shape[1]), f32))
    return jnp.concatenate(parts, axis=0).astype(bf16)


def mm(a, b):
    return jnp.dot(a, b, preferred_element_type=f32)


def apply_l(x, jac, ld, dj, width):
    part = [x[:, q * width:(q + 1) * width] for q in range(NQ)]
    damp = jac[18:19]
    d_press = mm(ld, split3(part[0]))
    mixed = []
    for r in range(3):
        w = jac[3 * r:3 * r + 1] * part[1]
        for d in range(1, 3):
            w = w + jac[3 * r + d:3 * r + d + 1] * part[1 + d]
        mixed.append(split3(w))
    diverg = mm(dj, jnp.concatenate(mixed, axis=0))[:BR]
    rates = [diverg - damp * part[0]]
    for d in range(3):
        g = jac[9 + d:10 + d] * d_press[:BR]
        for r in range(1, 3):
            g = g + jac[9 + 3 * r + d:10 + 3 * r + d] * d_press[r * BR:(r + 1) * BR]
        rates.append(g - damp * part[1 + d])
    return jnp.concatenate(rates, axis=1)


def combine(terms, start_time, end_time):
    total = None
    for w, t in zip(weights(start_time, end_time), terms):
        total = w * t if total is None else total + w * t
    return total


def traces(x, pf, width):
    t = mm(pf, split3(x))
    cols = []
    for f in range(4):
        rows = [t[f * KR:(f + 1) * KR, q * width:(q + 1) * width] for q in range(NQ)]
        cols.append(jnp.concatenate(rows, axis=0))
    return cols


def gather(x, onehot):
    hi, lo = hi_lo(x)
    out = mm(jnp.concatenate([hi, lo], axis=0).astype(bf16), onehot)
    n = x.shape[0]
    return out[:n] + out[n:]


def lift(jumps, coef, lf, width, stride):
    flux = [[] for _ in range(NQ)]
    for f in range(4):
        c = coef[:, f * stride:f * stride + width]
        jp = jumps[f][:KR]
        ju = [jumps[f][(1 + d) * KR:(2 + d) * KR] for d in range(3)]
        lam = c[6:7]
        g = c[0:1] * ju[0]
        for d in range(1, 3):
            g = g + c[d:d + 1] * ju[d]
        flux[0].append(g - lam * jp)
        for d in range(3):
            flux[1 + d].append(c[3 + d:4 + d] * jp - lam * ju[d])
    cat = jnp.concatenate([jnp.concatenate(fl, axis=0) for fl in flux], axis=1)
    return mm(lf, split3(cat))[:BR]


def block_mask(shape, block):
    return lax.broadcasted_iota(jnp.int32, shape, 1) // 32 == block


def turn(x, blocks):
    blocks %= 4
    return pltpu.roll(x, 32 * blocks, 1) if blocks else x


def write_parts(refs, sent):
    m_a, m_w, m_1, m_2, m_3, m_own = refs
    for i, ref in ((0, m_a), (1, m_w)):
        part = sent[:, i * LANES:(i + 1) * LANES]
        for q in range(3):
            row = part[q * KR:(q + 1) * KR]
            ref[q * KR:(q + 1) * KR] = jnp.where(block_mask(row.shape, 3), turn(part[3 * KR:], 3 - q), row)
    sub = sent[:, 2 * LANES:]
    for k, ref in ((1, m_1), (2, m_2), (3, m_3)):
        msg = turn(sub[:KR], -k)
        for q in range(1, NQ):
            msg = jnp.where(block_mask(msg.shape, q), turn(sub[q * KR:(q + 1) * KR], q - k), msg)
        ref[:KR] = msg
    m_own[...] = sub


def unpack(msg):
    last = turn(msg[2 * KR:], -1)
    for q in (1, 0):
        last = jnp.where(block_mask(last.shape, q), turn(msg[q * KR:(q + 1) * KR], q - 3), last)
    return jnp.concatenate([msg, last], axis=0)


def received(refs, inner):
    a, w, s1, s2, s3 = [refs[TAKEN.index(i)] for i in range(5)]
    own = refs[5][...]
    a = unpack(a[...])
    w = unpack(w[...])
    w = jnp.where(inner[0:1] > 0.5, w, jnp.zeros_like(w))
    s1, s2, s3 = s1[:KR], s2[:KR], s3[:KR]
    rows = []
    for q in range(NQ):
        row = own[q * KR:(q + 1) * KR]
        for k, msg in ((1, s1), (2, s2), (3, s3)):
            row = jnp.where(block_mask(row.shape, k), turn(msg, k - q), row)
        rows.append(row)
    return jnp.concatenate([a, w, jnp.concatenate(rows, axis=0)], axis=1)


def first_kernel(n_elem, n_dom, *refs):
    raw = refs[:13]
    (o_ld, o_dj, o_pf, o_norm, o_lift, o_nbr, o_jac, o_soh, o_in, o_xh, o_ph, o_x, o_x1, o_x2,
     o_x3, o_x4, o_t0, m_a, m_w, m_1, m_2, m_3, m_own) = refs[13:36]
    held, sem, pad, lists = list(refs[36:46]), refs[46], refs[47], refs[48]
    held.insert(2, o_norm)
    held.insert(7, o_lift)
    held.insert(10, o_nbr)
    copies = [
        pltpu.make_async_copy(src, dst, sem.at[i]) for i, (src, dst) in enumerate(zip(raw, held))
    ]
    for c in copies:
        c.start()
    (start, inv_jac, normals, bulk, density, deriv, proj, liftm, cluster, pml, neighbours,
     dom_send, sub_send) = held
    pad[...] = jnp.zeros_like(pad)
    o_x[...] = jnp.zeros_like(o_x)
    for c in copies:
        c.wait()
    dom_id, sub_id = lax.axis_index("dom"), lax.axis_index("sub")
    inner = jnp.logical_and(dom_id > 0, dom_id < n_dom - 1)
    o_in[...] = jnp.full(o_in.shape, jnp.where(inner, 1.0, 0.0).astype(f32), f32)
    for r in range(3):
        pad[r * BR:r * BR + NB, :NB] = deriv[r]
    hi, lo = hi_lo(pad[:3 * BR])
    left = hi + pltpu.roll(hi, BR, 1) + pltpu.roll(lo, 2 * BR, 1)
    zero8 = jnp.zeros((8, LANES), f32)
    ld = jnp.concatenate([left, zero8], axis=0).astype(bf16)
    dj = jnp.concatenate(
        [jnp.concatenate([left[r * BR:(r + 1) * BR], zero8], axis=0) for r in range(3)], axis=1
    ).astype(bf16)
    pad[...] = jnp.zeros_like(pad)
    for f in range(4):
        pad[f * KR:f * KR + NF, :NB] = proj[:, f, :]
    hi, lo = hi_lo(pad[:4 * KR])
    pf = (hi + pltpu.roll(hi, BR, 1) + pltpu.roll(lo, 2 * BR, 1)).astype(bf16)
    o_ld[...] = ld
    o_dj[...] = dj
    o_pf[...] = pf
    bulk_row = bulk[...].reshape(1, n_elem)
    dens_row = density[...].reshape(1, n_elem)
    fine = jnp.where(cluster[...].reshape(1, n_elem) == 1, 1.0, 0.0).astype(f32)
    damp = sigma_pml * pml[...].reshape(1, n_elem).astype(f32)
    jac_in = inv_jac[...]
    o_jac[0:9] = -bulk_row * jac_in
    o_jac[9:18] = -jac_in / dens_row
    o_jac[18:19] = damp
    o_jac[19:20] = fine
    o_jac[20:21] = bulk_row
    o_jac[21:22] = dens_row
    o_jac[22:24] = jnp.zeros((2, n_elem), f32)
    for q in range(NQ):
        o_x[:NB, q * n_elem:(q + 1) * n_elem] = start[q * NB:(q + 1) * NB]
    x = o_x[...]
    jac = o_jac[...]
    terms = [x]
    for ref in (o_x1, o_x2, o_x3, o_x4):
        terms.append(apply_l(terms[-1], jac, ld, dj, n_elem))
        ref[...] = terms[-1]
    p0 = combine(terms, 0.0, SUB_DT)
    o_xh[...] = head(x, n_elem)
    o_ph[...] = head(p0, n_elem)
    t0 = jnp.concatenate(traces(p0, pf, n_elem), axis=1)
    o_t0[...] = t0
    lists[...] = jnp.full(lists.shape, -1, jnp.int32)
    even = dom_id % 2 == 0
    before, after = dom_send[0:1], dom_send[1:2]
    n_halo = before.shape[1]
    lists[0:1, :n_halo] = jnp.where(even, after, before)
    lists[0:1, LANES:LANES + n_halo] = jnp.where(even, before, after)
    for b in range(4):
        lists[0:1, 2 * LANES + 32 * b:2 * LANES + 32 * (b + 1)] = sub_send[pl.ds(sub_id ^ b, 1)]
    names = lists[0:1]
    n_face = 4 * n_elem
    step = 256
    for j in range(0, n_face, step):
        row = j + lax.broadcasted_iota(jnp.int32, (step, 3 * LANES), 0)
        o_soh[j:j + step] = jnp.where(row == names, 1.0, 0.0).astype(bf16)
    write_parts((m_a, m_w, m_1, m_2, m_3, m_own), gather(t0, o_soh[...]))


def fine_base(state, pub, t, roh, coef, jac, ld, dj, lf, n_elem):
    tile = LANES
    got = gather(t, roh[:4 * n_elem])
    jumps = [
        got[:, f * tile:(f + 1) * tile] - t[:, f * n_elem:f * n_elem + tile] for f in range(4)
    ]
    corr = lift(jumps, coef, lf, tile, n_elem)
    return state + apply_l(pub, jac, ld, dj, tile) - corr


def head(x, n_elem):
    return jnp.concatenate(
        [x[:, q * n_elem:q * n_elem + LANES] for q in range(NQ)], axis=1
    )


def table(at, roh, n_elem, first, count):
    step = 128
    for f in range(4):
        col = at[f:f + 1, first:first + count]
        for j in range(0, roh.shape[0], step):
            row = j + lax.broadcasted_iota(jnp.int32, (step, count), 0)
            roh[j:j + step, f * count:(f + 1) * count] = jnp.where(row == col, 1.0, 0.0).astype(bf16)


def remap(nbr, n_elem, n_halo):
    n_face = 4 * n_elem
    even = lax.axis_index("dom") % 2 == 0
    sub_id = lax.axis_index("sub")
    before_at = jnp.where(even, n_face + LANES, n_face)
    after_at = jnp.where(even, n_face, n_face + LANES)
    slot = nbr - (n_face + 2 * n_halo)
    return jnp.where(
        nbr < n_face,
        nbr,
        jnp.where(
            nbr < n_face + n_halo,
            nbr - n_face + before_at,
            jnp.where(
                nbr < n_face + 2 * n_halo,
                nbr - (n_face + n_halo) + after_at,
                n_face + 2 * LANES + 32 * ((slot >> 5) ^ sub_id) + (slot & 31),
            ),
        ),
    )


def lift_setup(normals, liftm, jac, o_lf, o_coef, pad, n_elem):
    pad[...] = jnp.zeros_like(pad)
    for f in range(4):
        pad[f * KR:f * KR + NF, :NB] = liftm[:, f, :]
    full = jnp.transpose(pad[...])[:48]
    hi, lo = hi_lo(full)
    o_lf[...] = jnp.concatenate([hi + pltpu.roll(hi, 64, 1), lo], axis=1).astype(bf16)
    bulk_row, dens_row = jac[20:21], jac[21:22]
    speed = jnp.sqrt(bulk_row / dens_row)
    for f in range(4):
        n = normals[3 * f:3 * f + 3]
        lanes = pl.ds(f * n_elem, n_elem)
        o_coef[0:3, lanes] = 0.5 * bulk_row * n
        o_coef[3:6, lanes] = 0.5 * n / dens_row
        o_coef[6:7, lanes] = 0.5 * speed * jnp.sqrt(jnp.sum(n * n, axis=0, keepdims=True))
        o_coef[7:8, lanes] = jnp.zeros((1, n_elem), f32)


def coarse_traces(c, soh, jac, pf, o_t, o_s, n_elem):
    fine4 = jnp.concatenate([jac[19:20]] * 4, axis=1)
    t = jnp.concatenate(traces(c, pf[...], n_elem), axis=1)
    t = jnp.where(fine4 > 0.5, 0.0, t)
    o_t[...] = t
    o_s[...] = gather(t, soh[...])


def window0_kernel(n_elem, n_halo, nbr, normals, liftm, xh, ph, x, x1, x2, x3, x4, t0, soh, jac,
                   ld, dj, pf, roh, sfh, o_at, o_coef, o_lf, o_base, o_t1, o_s1, pad):
    for f in range(4):
        sfh[f * LANES:(f + 1) * LANES] = soh[f * n_elem:f * n_elem + LANES]
    lift_setup(normals, liftm, jac, o_lf, o_coef, pad, n_elem)
    o_at[...] = remap(nbr[...], n_elem, n_halo)
    table(o_at, roh, n_elem, 0, LANES)
    o_base[...] = fine_base(xh[...], ph[...], t0[...], roh, o_coef[...], jac[:, :LANES], ld[...],
                            dj[...], o_lf[...], n_elem)
    c = combine([t[...] for t in (x, x1, x2, x3, x4)], SUB_DT, 2 * SUB_DT)
    coarse_traces(c, soh, jac, pf, o_t1, o_s1, n_elem)


def step_kernel(n_elem, last,
                inner, r_a, r_w, r_1, r_2, r_3, r_own, base, p_sum, s_coarse,
                roh, sfh, coef, jac, ld, dj, pf, lf,
                *outs):
    o_sum, o_t, m_a, m_w, m_1, m_2, m_3, m_own = outs[:8]
    n_face = 4 * n_elem
    tile = LANES
    got = received((r_a, r_w, r_1, r_2, r_3, r_own), inner[...])
    got = gather(got, roh[n_face:])
    jumps = [got[:, f * tile:(f + 1) * tile] for f in range(4)]
    state = base[...] - lift(jumps, coef[...], lf[...], tile, n_elem)
    jac_h = jac[:, :tile]
    terms = [state]
    for _ in range(ORDER - 1):
        terms.append(apply_l(terms[-1], jac_h, ld[...], dj[...], tile))
    pub = combine(terms, 0.0, SUB_DT)
    total = p_sum[...] + pub
    o_sum[...] = total
    if not last:
        outs[8][...] = state
        outs[9][...] = pub
    fine = jac_h[19:20] > 0.5
    zero = jnp.zeros((4 * KR, tile), f32)
    fine_t = [jnp.where(fine, t, zero) for t in traces(total if last else pub, pf[...], tile)]
    fine_t = jnp.concatenate(fine_t, axis=1)
    o_t[...] = fine_t
    sent = s_coarse[...] + gather(fine_t, sfh[...])
    write_parts((m_a, m_w, m_1, m_2, m_3, m_own), sent)


def whole_traces(t_coarse, fine_t, n_elem):
    parts = []
    for f in range(4):
        c = t_coarse[:, f * n_elem:(f + 1) * n_elem]
        parts.append(c[:, :LANES] + fine_t[:, f * LANES:(f + 1) * LANES])
        parts.append(c[:, LANES:])
    return jnp.concatenate(parts, axis=1)


def window_kernel(n_elem, more, at, state, pub, t_c, t_f, x, x1, x2, x3, x4, roh, soh, coef, jac, ld,
                  dj, pf, lf, o_base, o_t, o_s, o_more):
    t = whole_traces(t_c, t_f, n_elem)
    o_base[...] = fine_base(state[...], pub[...], t, roh, coef[...], jac[:, :LANES], ld[...],
                            dj[...], lf[...], n_elem)
    terms = [r[...] for r in (x, x1, x2, x3, x4)]
    if more == "table":
        c = combine(terms, 2 * SUB_DT, 3 * SUB_DT)
        table(at, o_more, n_elem, LANES, n_elem - LANES)
    else:
        c = combine(terms, 0.0, step_size)
        o_more[...] = c
    coarse_traces(c, soh, jac, pf, o_t, o_s, n_elem)


def all_faces(x, roh, roh2, rows, n_elem):
    rest = n_elem - LANES
    one, two = gather(x, roh[rows]), gather(x, roh2[rows])
    return [
        jnp.concatenate(
            [one[:, f * LANES:(f + 1) * LANES], two[:, f * rest:(f + 1) * rest]], axis=1
        )
        for f in range(4)
    ]


def window3_kernel(n_elem, x, cs, total, t_c, t_f, roh, roh2, coef, jac, ld, dj, lf, o_base):
    fine = jac[19:20, :LANES] > 0.5
    parts = []
    for q in range(NQ):
        c = cs[:, q * n_elem:(q + 1) * n_elem]
        parts.append(jnp.where(fine, total[:, q * LANES:(q + 1) * LANES], c[:, :LANES]))
        parts.append(c[:, LANES:])
    pub = jnp.concatenate(parts, axis=1)
    tv = whole_traces(t_c, t_f, n_elem)
    rows = slice(0, 4 * n_elem)
    jumps = [
        g - tv[:, f * n_elem:(f + 1) * n_elem]
        for f, g in enumerate(all_faces(tv, roh, roh2, rows, n_elem))
    ]
    corr = lift(jumps, coef[...], lf[...], n_elem, n_elem)
    o_base[...] = x[...] + apply_l(pub, jac[...], ld[...], dj[...], n_elem) - corr


def last_kernel(n_elem, inner, r_a, r_w, r_1, r_2, r_3, r_own, base, roh, roh2, coef, lf, out):
    got = received((r_a, r_w, r_1, r_2, r_3, r_own), inner[...])
    rows = slice(4 * n_elem, 4 * n_elem + 3 * LANES)
    jumps = all_faces(got, roh, roh2, rows, n_elem)
    res = base[...] - lift(jumps, coef[...], lf[...], n_elem, n_elem)
    for q in range(NQ):
        out[q * NB:(q + 1) * NB] = res[:NB, q * n_elem:(q + 1) * n_elem]


def call(kernel, name, outs, args, scratch=(), raw=(), hbm_out=False, flops=0):
    vm = pl.BlockSpec(memory_space=pltpu.VMEM)
    specs, ops = [], []
    for i, a in enumerate(args):
        if i in raw:
            specs.append(pl.BlockSpec(memory_space=pltpu.HBM))
            ops.append(pltpu.with_memory_space_constraint(a, pltpu.HBM))
        else:
            specs.append(vm)
            ops.append(pltpu.with_memory_space_constraint(a, pltpu.VMEM))
    shapes = [
        jax.ShapeDtypeStruct(s, d) if hbm_out else pltpu.VMEM(s, d) for s, d in outs
    ]
    return pl.pallas_call(
        kernel,
        in_specs=specs,
        out_specs=[vm] * len(shapes),
        out_shape=shapes,
        scratch_shapes=list(scratch),
        name=name,
        compiler_params=pltpu.CompilerParams(vmem_limit_bytes=16 << 20),
        cost_estimate=pl.CostEstimate(flops=flops, bytes_accessed=1 << 16, transcendentals=0),
    )(*ops)


TAKEN = (4, 3, 1, 2, 0)


def exchange(parts, n_dom):
    a, w, s1, s2, s3, own = parts
    other = [(i, ((i + 1) ^ 1) - 1 if 0 < i < n_dom - 1 else n_dom - 1 - i) for i in range(n_dom)]
    r1 = lax.ppermute(s1, "sub", [(i, i ^ 1) for i in range(4)])
    ra = lax.ppermute(a, "dom", [(i, i ^ 1) for i in range(n_dom)])
    r3 = lax.ppermute(s3, "sub", [(i, i ^ 3) for i in range(4)])
    rw = lax.ppermute(w, "dom", other)
    r2 = lax.ppermute(s2, "sub", [(i, i ^ 2) for i in range(4)])
    got = (ra, rw, r1, r2, r3)
    return tuple(got[i] for i in TAKEN) + (own,)


def make_body(n_dom, n_sub):
    assert n_dom % 2 == 0 and n_sub == 4

    def body(start_dofs, inv_jac, normals, bulk_modulus, density, deriv_mats, face_proj, face_lift,
             cluster, pml_flags, neighbours, dom_send, sub_send):
        n_elem = start_dofs.shape[1]
        n_halo = dom_send.shape[1]
        assert n_halo <= 96
        n_face = 4 * n_elem
        wide = ((BR, NQ * n_elem), f32)
        slim = ((BR, NQ * LANES), f32)
        trace = ((4 * KR, n_face), f32)
        fine_trace = ((4 * KR, 4 * LANES), f32)
        listed = ((4 * KR, 3 * LANES), f32)
        msg = ((4 * KR, LANES), f32)
        small = ((KR, LANES), f32)
        dom_msg = ((3 * KR, LANES), f32)
        msg_row = ((8, LANES), f32)
        msgs = [dom_msg, dom_msg, dom_msg, small, small, msg]
        half = ((n_face + 3 * LANES, 4 * LANES), bf16)
        rest = ((n_face + 3 * LANES, 4 * (n_elem - LANES)), bf16)
        raw = [start_dofs, inv_jac, normals, bulk_modulus, density, deriv_mats,
               jnp.transpose(face_proj, (1, 0, 2)), jnp.transpose(face_lift, (2, 0, 1)),
               cluster, pml_flags, neighbours, dom_send, sub_send]
        first = call(
            lambda *r: first_kernel(n_elem, n_dom, *r), "first",
            [((128, 128), bf16), ((48, 384), bf16), ((64, 128), bf16)]
            + [(raw[i].shape, raw[i].dtype) for i in (2, 7, 10)]
            + [((24, n_elem), f32), ((n_face, 3 * LANES), bf16), msg_row, slim, slim]
            + [wide] * 5 + [trace] + msgs,
            raw, raw=range(13),
            scratch=[pltpu.VMEM(a.shape, a.dtype) for i, a in enumerate(raw) if i not in (2, 7, 10)]
            + [pltpu.SemaphoreType.DMA((len(raw),)), pltpu.VMEM((128, LANES), f32),
               pltpu.VMEM((8, 3 * LANES), jnp.int32)],
        )
        ld, dj, pf, norm, liftm, nbr, jac, soh, inner, xh, total, *terms, t = first[:17]
        got = exchange(first[17:], n_dom)
        roh, sfh, at, coef, lf, base, t_c, s_c = call(
            lambda *r: window0_kernel(n_elem, n_halo, *r), "window0",
            [half, ((4 * LANES, 3 * LANES), bf16), ((4, n_elem), jnp.int32), ((8, n_face), f32), ((48, 256), bf16), slim, trace,
             listed],
            [nbr, norm, liftm, xh, total, *terms, t, soh, jac, ld, dj, pf],
            scratch=[pltpu.VMEM((LANES, LANES), f32)], flops=1 << 36,
        )
        roh2 = cs = None
        for s in range(SUBSTEPS - 1):
            last = s == SUBSTEPS - 2
            outs = call(
                lambda *r, last=last: step_kernel(n_elem, last, *r), "step",
                [slim, fine_trace] + msgs + ([] if last else [slim] * 2),
                [inner, *got, base, total, s_c, roh, sfh, coef, jac, ld, dj, pf, lf],
            )
            total, t = outs[:2]
            got = exchange(outs[2:8], n_dom)
            if last:
                (base,) = call(
                    lambda *r: window3_kernel(n_elem, *r), "window3", [wide],
                    [terms[0], cs, total, t_c, t, roh, roh2, coef, jac, ld, dj, lf], flops=1 << 36,
                )
            else:
                more = ("table", "sum")[s]
                base, t_c, s_c, extra = call(
                    lambda *r, more=more: window_kernel(n_elem, more, *r), "window",
                    [slim, trace, listed, rest if s == 0 else wide],
                    [at, outs[8], outs[9], t_c, t, *terms, roh, soh, coef, jac, ld, dj, pf, lf],
                    flops=1 << 36,
                )
                if s == 0:
                    roh2 = extra
                else:
                    cs = extra
        (out,) = call(
            lambda *r: last_kernel(n_elem, *r), "last",
            [((NQ * NB, n_elem), f32)], [inner, *got, base, roh, roh2, coef, lf], hbm_out=True,
        )
        return out

    return body


def solution(mesh):
    in_specs = (
        P(None, ("dom", "sub")),
        P(None, ("dom", "sub")),
        P(None, ("dom", "sub")),
        P(("dom", "sub")),
        P(("dom", "sub")),
        P(),
        P(),
        P(),
        P(("dom", "sub")),
        P(("dom", "sub")),
        P(None, ("dom", "sub")),
        P(("dom", "sub"), None),
        P(("dom", "sub"), None),
    )
    out_specs = P(None, ("dom", "sub"))
    body = make_body(mesh.shape["dom"], mesh.shape["sub"])
    return jax.shard_map(body, mesh=mesh, in_specs=in_specs, out_specs=out_specs, check_vma=False)
```
